512 devices in a mesh: front: 4 (over x), row: 8 (over y), col: 16 (over z, core).
Axes of the slice: x: 4, y: 8, z: 8, core: 2. Of those that a mesh axis runs over, the one named last changes fastest.
Arguments:
- contrib: float32 [32768, 4096], P(('front', 'row'), 'col'), parts along dimension 0, as said below
- front_diag: float32 [32768], P(('front', 'row')), parts along dimension 0, may hold values from 1 to 4
- child_map: int32 [8, 32], P('front'), parts along dimension 0, may hold values from 0 to 63, as said below
- pivots: int32 [16], P('front'), parts along dimension 0, may hold values from 0 to 63, as said below
Outputs:
- lfactor: float32 [32768, 512], P(('front', 'row'), 'col'), parts along dimension 0
- schur_block: float32 [32768, 8192], P(('front', 'row'), 'col'), parts along dimension 0
The draws below stay inside these ranges and needn't reach their ends.
There are 4 independent parts, one for each index of `front`. The reference program is written for one: setup_inputs(seed, part) draws one part's arguments, and reference() takes and returns one part's arrays. A program takes and returns all parts, laid end to end along the dimension named above; each array names one. Nothing has to cross between parts.
Inputs may be any that keep to these rules, and one draw needn't show every extreme that they name: child_map[c, b] is b or b + 32, chosen for each child and block. `pivots`: 4 distinct front blocks. `contrib`: each child's contribution block is symmetric positive definite.
All inputs are finite; a program needn't handle non-finite values.
Results may differ from the reference program's by a relative error of at most 0.0001.
Values sent between devices are 32-bit elements; how exact they have to be, the bound alone decides.
A program may use at most 64 MiB of HBM per device.

```python
import math
import jax
import jax.numpy as jnp
from jax import lax

NF = 8192
NB = 64
NPAN = 2
BLK = 128
CB = 4096
CBB = 32
NPB = 4
N_ROW = 8
N_COL = 16


def stored_rows(values, device_count):
    length = values.shape[0]
    reshaped = values.reshape((length // (device_count * BLK), device_count, BLK) + values.shape[1:])
    return jnp.swapaxes(reshaped, 0, 1).reshape(values.shape)


def child_matrix(child_key):
    subkeys = jax.random.split(child_key, 4)
    places = jax.random.permutation(subkeys[0], CB).astype(jnp.float32)
    reach = 2.0
    scales = jnp.exp(jax.random.uniform(subkeys[1], (CB,), jnp.float32, math.log(0.5), math.log(2.0)))
    dominant = 2.0 * jax.random.uniform(subkeys[3], (CB,), jnp.float32, 1.02, 1.5)
    kernel = scales[:, None] * scales[None, :] * jnp.exp(-jnp.abs(places[:, None] - places[None, :]) / reach)
    rough = jax.random.uniform(subkeys[2], (CB, CB), jnp.float32, -1.0, 1.0) * (2.0 / CB)
    rough = 0.5 * (rough + rough.T) * (1.0 - jnp.eye(CB, dtype=jnp.float32))
    return kernel + rough + jnp.diag(dominant)


def draw_contrib(key, part):
    halves = []
    for child_index in range(2):
        matrix = child_matrix(jax.random.fold_in(key, 101 + child_index))
        matrix = stored_rows(matrix, N_ROW // 2)
        matrix = stored_rows(matrix.T, N_COL).T
        halves.append(matrix)
    return jnp.concatenate(halves, axis=0)


def draw_child_map(key, part):
    upper = jax.random.randint(jax.random.fold_in(key, 7), (2, CBB), 0, 2)
    upper = upper.at[0, 0].set(0).at[0, CBB - 1].set(1)
    return (jnp.arange(CBB, dtype=jnp.int32)[None, :] + CBB * upper).astype(jnp.int32)


def draw_pivots(key, part):
    shuffled = jax.random.permutation(jax.random.fold_in(key, 13), NB)
    return shuffled[:NPB].astype(jnp.int32)


def block_levels(key, extent, pieces, smallest, largest):
    loudness, own = 1.0, jax.random.fold_in(key, 6)
    for axis_at, parts in pieces:
        draws = jnp.exp(jax.random.uniform(jax.random.fold_in(own, axis_at), (parts,), jnp.float32, smallest / len(pieces), largest / len(pieces)))
        loudness = loudness * jnp.repeat(draws, extent[axis_at] // parts).reshape([-1 if axis == axis_at else 1 for axis in range(len(extent))])
    return loudness


def setup_inputs(seed: int = 0, part: int = 0) -> dict:
    streams_of = jax.random.split(jax.random.key(seed), 5)
    part_splits = jax.random.split(jax.random.fold_in(streams_of[4], part), 5)
    contrib = draw_contrib(jax.random.fold_in(jax.random.fold_in(streams_of[4], part), 71), part)
    front_diag = jnp.clip(1.0 + 3.0 * jax.random.uniform(part_splits[1], (NF,), jnp.float32) ** block_levels(part_splits[1], (NF,), ((0, 8),), -0.2, 0.2), 1.0, 4.0)
    child_map = draw_child_map(jax.random.fold_in(jax.random.fold_in(streams_of[4], part), 71), part)
    pivots = draw_pivots(jax.random.fold_in(jax.random.fold_in(streams_of[4], part), 71), part)
    return {"contrib": contrib, "front_diag": front_diag, "child_map": child_map, "pivots": pivots}


def rows_to_logical(values, device_count):
    length = values.shape[0]
    reshaped = values.reshape((device_count, length // (device_count * BLK), BLK) + values.shape[1:])
    return jnp.swapaxes(reshaped, 0, 1).reshape(values.shape)

def rows_to_stored(values, device_count):
    length = values.shape[0]
    reshaped = values.reshape((length // (device_count * BLK), device_count, BLK) + values.shape[1:])
    return jnp.swapaxes(reshaped, 0, 1).reshape(values.shape)

def reference(contrib, front_diag, child_map, pivots):
    half_rows = N_ROW // 2
    blocks = jnp.zeros((NB, NB, BLK, BLK), jnp.float32)
    for child_index in range(2):
        child_part = contrib[child_index * CB:(child_index + 1) * CB]
        child_part = rows_to_logical(child_part, half_rows)
        child_part = rows_to_logical(child_part.T, N_COL).T
        child_tiles = child_part.reshape(CBB, BLK, CBB, BLK).transpose(0, 2, 1, 3)
        target_ids = child_map[child_index]
        blocks = blocks.at[target_ids[:, None], target_ids[None, :]].add(child_tiles)
    front_matrix = blocks.transpose(0, 2, 1, 3).reshape(NF, NF)
    front_matrix = front_matrix + jnp.diag(rows_to_logical(front_diag, N_ROW))
    offsets = jnp.arange(BLK, dtype=jnp.int32)
    factor_list = []
    for panel_index in range(NPAN):
        pivot_ids = jnp.concatenate([pivots[2 * panel_index] * BLK + offsets, pivots[2 * panel_index + 1] * BLK + offsets]).astype(jnp.int32)
        panel_cols = jnp.take(front_matrix, pivot_ids, axis=1)
        pivot_block = jnp.take(panel_cols, pivot_ids, axis=0)
        lower_factor = jnp.linalg.cholesky(pivot_block)
        factor = lax.linalg.triangular_solve(lower_factor, panel_cols, left_side=False, lower=True, transpose_a=True)
        front_matrix = front_matrix - jnp.dot(factor.astype(jnp.float32), factor.T.astype(jnp.float32), precision=lax.Precision.HIGHEST, preferred_element_type=jnp.float32)
        keep_mask = jnp.ones((NF,), jnp.float32).at[pivot_ids].set(0.0)
        front_matrix = front_matrix * keep_mask[:, None] * keep_mask[None, :]
        factor_list.append(factor)
    lfactor = rows_to_stored(jnp.concatenate(factor_list, axis=1), N_ROW)
    schur_block = rows_to_stored(rows_to_stored(front_matrix, N_ROW).T, N_COL).T
    return (lfactor, schur_block)
```

```python
import jax
import jax.numpy as jnp
from jax import lax
from jax.experimental import pallas as pl
from jax.experimental.pallas import tpu as pltpu
from jax.sharding import PartitionSpec as P

F32 = jnp.float32
HIGHEST = lax.Precision.HIGHEST
MESH = pl.DeviceIdType.MESH
B = 128
LOWER = [4 * p + q for p in range(4) for q in range(p + 1)]


def dot(a, b, ca, cb):
    return lax.dot_general(
        a, b, (((ca,), (cb,)), ((), ())), precision=HIGHEST, preferred_element_type=F32
    )


def gather_kernel(
    pv, cm, con_ref, fd_ref, af_ref, pc_ref, pr_ref,
    cand, rsb, g, acand, ra, ab,
    ss_a, rs_a, ss_b, rs_b, ss_c, rs_c, ss_d, rs_d, ss_e, rs_e, ss_f, rs_f,
):
    f = lax.axis_index("front")
    r = lax.axis_index("row")
    c = lax.axis_index("col")
    s = r // 4
    d = r % 4

    def copy(src, dst, ssem, rsem, row, col):
        return pltpu.make_async_remote_copy(
            src_ref=src, dst_ref=dst, send_sem=ssem, recv_sem=rsem,
            device_id=(f, row, col), device_id_type=MESH,
        )

    barrier = pltpu.get_barrier_semaphore()
    for k in range(1, 8):
        pl.semaphore_signal(barrier, inc=1, device_id=(f, (r + k) % 8, c), device_id_type=MESH)
    for k in range(1, 16):
        pl.semaphore_signal(barrier, inc=1, device_id=(f, r, (c + k) % 16), device_id_type=MESH)

    cand[:, 64:72, :] = jnp.zeros((8, 8, 256), F32)
    for p in range(4):
        b = pv[p] % 32
        mine = jnp.logical_and(cm[s, b] == pv[p], b % 4 == d)
        rows = con_ref[pl.ds((b // 4) * B, B), :]
        rows = jnp.where(mine, rows, 0.0)
        cand[:, p * 16:(p + 1) * 16, :] = rows.reshape(8, 16, 256)
        line = fd_ref[pl.ds(pv[p] // 8, 1), :]
        line = jnp.where(pv[p] % 8 == r, line, 0.0)
        cand[:, 64 + p:65 + p, 0:B] = jnp.broadcast_to(line[None], (8, 1, B))
    rsb[r] = cand[r]

    pl.semaphore_wait(barrier, 22)

    first = []
    for k in range(1, 8):
        to = (r + k) % 8
        cp = copy(cand.at[to], rsb.at[r], ss_a.at[k], rs_a.at[r], to, c)
        cp.start()
        first.append(cp)
    for k in range(1, 8):
        frm = (r + 8 - k) % 8
        copy(cand.at[frm], rsb.at[frm], ss_a.at[k], rs_a.at[frm], frm, c).wait_recv()

    lane = lax.broadcasted_iota(jnp.int32, (16, B), 1)
    sub = lax.broadcasted_iota(jnp.int32, (16, B), 0)
    on_diag = lane == sub + 16 * r
    sums = []
    for ch in range(2):
        sums.append(
            (rsb[4 * ch, 0:64, :] + rsb[4 * ch + 1, 0:64, :])
            + (rsb[4 * ch + 2, 0:64, :] + rsb[4 * ch + 3, 0:64, :])
        )
    diag = rsb[0, 64:72, 0:B]
    for k in range(1, 8):
        diag = diag + rsb[k, 64:72, 0:B]
    for p in range(4):
        dp = jnp.where(on_diag, jnp.broadcast_to(diag[p:p + 1, :], (16, B)), 0.0)
        for l in range(4):
            i = l % 2
            total = jnp.where(16 * l + c == pv[p], dp, 0.0)
            for ch in range(2):
                here = cm[ch, 16 * i + c] == 16 * l + c
                part = sums[ch][p * 16:(p + 1) * 16, i * B:(i + 1) * B]
                total = total + jnp.where(here, part, 0.0)
            g[p, l] = total

    pc_ref[r] = g[...]
    gathers = []
    for k in range(1, 8):
        to = (r + k) % 8
        cp = copy(g, pc_ref.at[r], ss_e.at[k], rs_e.at[r], to, c)
        gathers.append(cp)

    for p in range(4):
        for q in range(p + 1):
            total = jnp.zeros((16, B), F32)
            for l in range(4):
                total = total + jnp.where(16 * l + c == pv[q], g[p, l], 0.0)
            acand[4 * p + q] = total
    for m in LOWER:
        @pl.when(c != m)
        def _():
            copy(acand.at[m], ra.at[c], ss_b.at[m], rs_b.at[c], r, m).start()

        @pl.when(c == m)
        def _():
            ra[m] = acand[m]
    for cp in gathers:
        cp.start()
    member = c % 4 <= c // 4

    @pl.when(member)
    def _():
        for n in range(16):
            @pl.when(c != n)
            def _():
                copy(acand.at[0], ra.at[n], ss_b.at[0], rs_b.at[n], r, n).wait_recv()
        ab[r] = jnp.sum(ra[...], axis=0)
        for k in range(1, 8):
            to = (r + k) % 8
            copy(ab.at[r], ab.at[r], ss_c.at[k], rs_c.at[r], to, c).start()
        for k in range(1, 8):
            frm = (r + 8 - k) % 8
            copy(ab.at[r], ab.at[frm], ss_c.at[k], rs_c.at[frm], frm, c).wait_recv()
        af_ref[c] = ab[...]
        for k in range(1, 16):
            to = (c + k) % 16
            copy(ab, af_ref.at[c], ss_d.at[k], rs_d.at[c], r, to).start()

    z = c // 2
    o = (z - r // 2 + 8) % 8
    relay = c % 2 == r % 2
    right = (c + 2) % 16
    left = (c + 14) % 16
    twin = c + 1 - 2 * (c % 2)

    def hop(h, k, src, do_right, do_left):
        @pl.when(do_right)
        def _():
            copy(src, pr_ref.at[h, k], ss_f.at[h, k, 0], rs_f.at[h, k], r, right).start()

        @pl.when(do_left)
        def _():
            copy(src, pr_ref.at[h, k], ss_f.at[h, k, 1], rs_f.at[h, k], r, left).start()

        copy(src, pr_ref.at[h, k], ss_f.at[h, k, 2], rs_f.at[h, k], r, twin).start()

    def wait_pr(h, k):
        copy(g, pr_ref.at[h, k], ss_f.at[h, k, 2], rs_f.at[h, k], r, twin).wait_recv()

    for k in range(8):
        @pl.when(r != k)
        def _():
            copy(g, pc_ref.at[k], ss_e.at[0], rs_e.at[k], r, c).wait_recv()

        @pl.when(relay)
        def _():
            for h in range(2):
                oh = (o + 8 - 4 * h) % 8

                @pl.when(oh == 0)
                def _():
                    pr_ref[h, k] = pc_ref[k]

                @pl.when(oh != 0)
                def _():
                    wait_pr(h, k)

                hop(h, k, pr_ref.at[h, k], oh <= 3, jnp.logical_or(oh == 0, oh >= 6))

    @pl.when(jnp.logical_not(relay))
    def _():
        for k in range(8):
            for h in range(2):
                wait_pr(h, k)

    for m in LOWER:
        @pl.when(c != m)
        def _():
            copy(ab, af_ref.at[m], ss_d.at[0], rs_d.at[m], r, m).wait_recv()
            copy(acand.at[m], ra.at[c], ss_b.at[m], rs_b.at[c], r, m).wait_send()
    for cp in first:
        cp.wait_send()
    for cp in gathers:
        cp.wait_send()

    @pl.when(member)
    def _():
        for k in range(1, 8):
            copy(ab.at[r], ab.at[r], ss_c.at[k], rs_c.at[r], (r + k) % 8, c).wait_send()
        for k in range(1, 16):
            copy(ab, af_ref.at[c], ss_d.at[k], rs_d.at[c], r, (c + k) % 16).wait_send()

    @pl.when(relay)
    def _():
        for k in range(8):
            for h in range(2):
                oh = (o + 8 - 4 * h) % 8

                @pl.when(oh <= 3)
                def _():
                    copy(g, pr_ref.at[h, k], ss_f.at[h, k, 0], rs_f.at[h, k], r, right).wait_send()

                @pl.when(jnp.logical_or(oh == 0, oh >= 6))
                def _():
                    copy(g, pr_ref.at[h, k], ss_f.at[h, k, 1], rs_f.at[h, k], r, left).wait_send()

                copy(g, pr_ref.at[h, k], ss_f.at[h, k, 2], rs_f.at[h, k], r, twin).wait_send()


def gather(pv, cm, contrib, fd):
    dma = pltpu.SemaphoreType.DMA
    vm = pl.BlockSpec(memory_space=pltpu.VMEM)
    sm = pl.BlockSpec(memory_space=pltpu.SMEM)
    return pl.pallas_call(
        gather_kernel,
        out_shape=(
            jax.ShapeDtypeStruct((16, 8, 16, B), F32),
            jax.ShapeDtypeStruct((8, 4, 4, 16, B), F32),
            jax.ShapeDtypeStruct((2, 8, 4, 4, 16, B), F32),
        ),
        in_specs=[sm, sm, vm, vm],
        out_specs=(vm, vm, vm),
        scratch_shapes=[
            pltpu.VMEM((8, 72, 256), F32),
            pltpu.VMEM((8, 72, 256), F32),
            pltpu.VMEM((4, 4, 16, B), F32),
            pltpu.VMEM((16, 16, B), F32),
            pltpu.VMEM((16, 16, B), F32),
            pltpu.VMEM((8, 16, B), F32),
            dma((8,)), dma((8,)), dma((16,)), dma((16,)), dma((8,)), dma((8,)),
            dma((16,)), dma((16,)), dma((8,)), dma((8,)), dma((2, 8, 3)), dma((2, 8)),
        ],
        compiler_params=pltpu.CompilerParams(
            collective_id=0, has_side_effects=True, vmem_limit_bytes=40 << 20
        ),
        name="gather",
    )(pv, cm, contrib, fd)


def factor_block(w_ref, r_ref, out_ref):
    row = lax.broadcasted_iota(jnp.int32, (16, 8, B), 0) * 8 + lax.broadcasted_iota(
        jnp.int32, (16, 8, B), 1
    )
    col = lax.broadcasted_iota(jnp.int32, (16, 8, B), 2)
    r_ref[...] = jnp.where(row == col, 1.0, 0.0).astype(F32)
    for t in range(16):
        w = w_ref[t]
        v = r_ref[t]
        cols = [jnp.broadcast_to(w[:, 8 * t + k:8 * t + k + 1], (8, B)) for k in range(8)]
        a = [[None] * 8 for _ in range(8)]
        for k in range(8):
            for i in range(k, 8):
                a[i][k] = jnp.broadcast_to(cols[k][i:i + 1, :], (8, B))
        wr = [jnp.broadcast_to(w[i:i + 1, :], (8, B)) for i in range(8)]
        vr = [jnp.broadcast_to(v[i:i + 1, :], (8, B)) for i in range(8)]
        rs = [None] * 8
        l = [[None] * 8 for _ in range(8)]
        for k in range(8):
            rs[k] = lax.rsqrt(a[k][k])
            for i in range(k + 1, 8):
                l[i][k] = a[i][k] * rs[k]
            for j in range(k + 1, 8):
                for i in range(j, 8):
                    a[i][j] = a[i][j] - l[i][k] * l[j][k]
            wr[k] = wr[k] * rs[k]
            vr[k] = vr[k] * rs[k]
            for i in range(k + 1, 8):
                wr[i] = wr[i] - l[i][k] * wr[k]
                vr[i] = vr[i] - l[i][k] * vr[k]
        for k in range(8):
            out_ref[8 * t + k:8 * t + k + 1, :] = vr[k][0:1, :]
        if t < 15:
            for k in range(7, -1, -1):
                for i in range(k + 1, 8):
                    wr[k] = wr[k] - l[i][k] * wr[i]
                    vr[k] = vr[k] - l[i][k] * vr[i]
                wr[k] = wr[k] * rs[k]
                vr[k] = vr[k] * rs[k]
            for u in range(t + 1, 16):
                old = w_ref[u]
                new = old
                inv = r_ref[u]
                for k in range(8):
                    factor = jnp.broadcast_to(old[:, 8 * t + k:8 * t + k + 1], (8, B))
                    new = new - factor * wr[k]
                    inv = inv - factor * vr[k]
                w_ref[u] = new
                r_ref[u] = inv


def cholesky_kernel(a_ref, l_ref, w_ref, r_ref):
    l_ref[...] = a_ref[...]

    def body(p, carry):
        w_ref[...] = l_ref[p, p].reshape(16, 8, B)
        factor_block(w_ref, r_ref, l_ref.at[p, p])
        inv = l_ref[p, p]

        def column(i, carry):
            @pl.when(i > p)
            def _():
                l_ref[i, p] = dot(l_ref[i, p], inv, 1, 1)
            return carry

        lax.fori_loop(0, 4, column, 0)

        def update(ij, carry):
            i = ij // 4
            j = ij % 4

            @pl.when(jnp.logical_and(j > p, i >= j))
            def _():
                l_ref[i, j] = l_ref[i, j] - dot(l_ref[i, p], l_ref[j, p], 1, 1)
            return carry

        lax.fori_loop(0, 16, update, 0)
        return carry

    lax.fori_loop(0, 4, body, 0)


def cholesky(a):
    vm = pl.BlockSpec(memory_space=pltpu.VMEM)
    return pl.pallas_call(
        cholesky_kernel,
        out_shape=jax.ShapeDtypeStruct((4, 4, B, B), F32),
        in_specs=[vm],
        out_specs=vm,
        scratch_shapes=[pltpu.VMEM((16, 8, B), F32)] * 2,
        name="cholesky",
        cost_estimate=pl.CostEstimate(flops=200_000_000, bytes_accessed=100_000_000, transcendentals=0),
    )(a)


def finish_kernel(pv, cm, pos, con_ref, x_ref, fd_ref, l_ref, pc_ref, pr_ref, lf_ref, s_ref, lt):
    r = pos[0]
    c = pos[1]
    s = r // 4
    for p in range(4):
        for k in range(8):
            blk = pr_ref[k % 2, :, p, k // 2].reshape(B, B)
            if p >= 2:
                gone = jnp.logical_or(8 * k + r == pv[0], 8 * k + r == pv[1])
                blk = jnp.where(gone, 0.0, blk)
            lt[p, :, k * B:(k + 1) * B] = blk
        for l in range(4):
            blk = pc_ref[:, p, l].reshape(B, B)
            lt[p, :, 1024 + l * B:1024 + (l + 1) * B] = blk
    for p in range(4):
        acc = lt[p]
        for q in range(p):
            acc = acc - dot(l_ref[p, q], lt[q], 1, 0)
        lt[p] = dot(l_ref[p, p], acc, 1, 0)
        if p >= 2:
            for k in range(8):
                gone = jnp.logical_or(8 * k + r == pv[0], 8 * k + r == pv[1])

                @pl.when(gone)
                def _():
                    lt[p, :, k * B:(k + 1) * B] = jnp.zeros((B, B), F32)
    mine = lt[c // 4, pl.ds(pl.multiple_of((c % 4) * 32, 32), 32), 0:1024]
    lf_ref[...] = mine.T
    row = lax.broadcasted_iota(jnp.int32, (B, B), 0)
    col = lax.broadcasted_iota(jnp.int32, (B, B), 1)
    for k in range(8):
        m = k % 4
        low = lt[:, :, k * B:(k + 1) * B].reshape(512, B)
        upd = dot(low, lt[:, :, 1024:1536].reshape(512, 512), 0, 0)
        own = con_ref[pl.ds(pl.multiple_of((2 * m + s) * B, B), B), :]
        other = x_ref[m]
        row_gone = jnp.zeros((), jnp.bool_)
        for p in range(4):
            row_gone = jnp.logical_or(row_gone, 8 * k + r == pv[p])
        own_row = cm[s, 8 * m + r] == 8 * k + r
        other_row = cm[1 - s, 8 * m + r] == 8 * k + r
        for l in range(4):
            i = l % 2
            front_col = 16 * l + c
            gone = row_gone
            for p in range(4):
                gone = jnp.logical_or(gone, front_col == pv[p])
            own_here = jnp.logical_and(own_row, cm[s, 16 * i + c] == front_col)
            other_here = jnp.logical_and(other_row, cm[1 - s, 16 * i + c] == front_col)
            tile = jnp.where(own_here, own[:, i * B:(i + 1) * B], 0.0)
            tile = tile + jnp.where(other_here, other[:, i * B:(i + 1) * B], 0.0)
            dk = jnp.where(row == col, jnp.broadcast_to(fd_ref[k:k + 1, :], (B, B)), 0.0)
            tile = tile + jnp.where(8 * k + r == front_col, dk, 0.0)
            tile = tile - upd[:, l * B:(l + 1) * B]
            s_ref[k * B:(k + 1) * B, l * B:(l + 1) * B] = jnp.where(gone, 0.0, tile)


def finish(pv, cm, pos, contrib, other, fd, low, pc, pr):
    vm = pl.BlockSpec(memory_space=pltpu.VMEM)
    sm = pl.BlockSpec(memory_space=pltpu.SMEM)
    return pl.pallas_call(
        finish_kernel,
        out_shape=(
            jax.ShapeDtypeStruct((1024, 32), F32),
            jax.ShapeDtypeStruct((1024, 512), F32),
        ),
        in_specs=[sm, sm, sm] + [vm] * 6,
        out_specs=(vm, vm),
        scratch_shapes=[pltpu.VMEM((4, B, 1536), F32)],
        compiler_params=pltpu.CompilerParams(vmem_limit_bytes=40 << 20),
        name="finish",
        cost_estimate=pl.CostEstimate(flops=1_000_000_000, bytes_accessed=8_000_000, transcendentals=0),
    )(pv, cm, pos, contrib, other, fd, low, pc, pr)


def per_device(contrib, front_diag, child_map, pivots):
    r = lax.axis_index("row")
    c = lax.axis_index("col")
    fd = front_diag.reshape(8, B)
    af, pc, pr = gather(pivots, child_map, contrib, fd)
    halves = contrib.reshape(4, 2, B, 256)
    away = lax.dynamic_index_in_dim(halves, 1 - r // 4, 1, keepdims=False)
    away, af = lax.optimization_barrier((away, af))
    other = lax.ppermute(away, "row", [(i, i ^ 4) for i in range(8)])
    low = cholesky(af.reshape(4, 4, B, B))
    pos = jnp.stack([r, c]).astype(jnp.int32)
    return finish(pivots, child_map, pos, contrib, other, fd, low, pc, pr)


def solution(mesh):
    placed = (P(("front", "row"), "col"), P(("front", "row")), P("front", None), P("front"))
    return jax.shard_map(
        per_device,
        mesh=mesh,
        in_specs=placed,
        out_specs=(P(("front", "row"), "col"), P(("front", "row"), "col")),
        check_vma=False,
    )
```

```python
import jax
import jax.numpy as jnp
from jax import lax
from jax.experimental import pallas as pl
from jax.experimental.pallas import tpu as pltpu
from jax.sharding import PartitionSpec as P

F32 = jnp.float32
HIGHEST = lax.Precision.HIGHEST
MESH = pl.DeviceIdType.MESH
B = 128
LOWER = [4 * p + q for p in range(4) for q in range(p + 1)]


def dot(a, b, ca, cb):
    return lax.dot_general(
        a, b, (((ca,), (cb,)), ((), ())), precision=HIGHEST, preferred_element_type=F32
    )


def gather_kernel(
    pv, cm, con_ref, fd_ref, af_ref, pc_ref, pr_ref,
    cand, rsb, g, acand, ra, ab,
    ss_a, rs_a, ss_b, rs_b, ss_c, rs_c, ss_d, rs_d, ss_e, rs_e, ss_f, rs_f,
):
    f = lax.axis_index("front")
    r = lax.axis_index("row")
    c = lax.axis_index("col")
    s = r // 4
    d = r % 4

    def copy(src, dst, ssem, rsem, row, col):
        return pltpu.make_async_remote_copy(
            src_ref=src, dst_ref=dst, send_sem=ssem, recv_sem=rsem,
            device_id=(f, row, col), device_id_type=MESH,
        )

    barrier = pltpu.get_barrier_semaphore()
    for k in range(1, 8):
        pl.semaphore_signal(barrier, inc=1, device_id=(f, (r + k) % 8, c), device_id_type=MESH)
    for k in range(1, 16):
        pl.semaphore_signal(barrier, inc=1, device_id=(f, r, (c + k) % 16), device_id_type=MESH)

    cand[:, 64:72, :] = jnp.zeros((8, 8, 256), F32)
    for p in range(4):
        b = pv[p] % 32
        mine = jnp.logical_and(cm[s, b] == pv[p], b % 4 == d)
        rows = con_ref[pl.ds((b // 4) * B, B), :]
        rows = jnp.where(mine, rows, 0.0)
        cand[:, p * 16:(p + 1) * 16, :] = rows.reshape(8, 16, 256)
        line = fd_ref[pl.ds(pv[p] // 8, 1), :]
        line = jnp.where(pv[p] % 8 == r, line, 0.0)
        cand[:, 64 + p:65 + p, 0:B] = jnp.broadcast_to(line[None], (8, 1, B))
    rsb[r] = cand[r]

    pl.semaphore_wait(barrier, 22)

    first = []
    for k in range(1, 8):
        to = (r + k) % 8
        cp = copy(cand.at[to], rsb.at[r], ss_a.at[k], rs_a.at[r], to, c)
        cp.start()
        first.append(cp)
    for k in range(1, 8):
        frm = (r + 8 - k) % 8
        copy(cand.at[frm], rsb.at[frm], ss_a.at[k], rs_a.at[frm], frm, c).wait_recv()

    lane = lax.broadcasted_iota(jnp.int32, (16, B), 1)
    sub = lax.broadcasted_iota(jnp.int32, (16, B), 0)
    on_diag = lane == sub + 16 * r
    sums = []
    for ch in range(2):
        sums.append(
            (rsb[4 * ch, 0:64, :] + rsb[4 * ch + 1, 0:64, :])
            + (rsb[4 * ch + 2, 0:64, :] + rsb[4 * ch + 3, 0:64, :])
        )
    diag = rsb[0, 64:72, 0:B]
    for k in range(1, 8):
        diag = diag + rsb[k, 64:72, 0:B]
    for p in range(4):
        dp = jnp.where(on_diag, jnp.broadcast_to(diag[p:p + 1, :], (16, B)), 0.0)
        for l in range(4):
            i = l % 2
            total = jnp.where(16 * l + c == pv[p], dp, 0.0)
            for ch in range(2):
                here = cm[ch, 16 * i + c] == 16 * l + c
                part = sums[ch][p * 16:(p + 1) * 16, i * B:(i + 1) * B]
                total = total + jnp.where(here, part, 0.0)
            g[p, l] = total

    pc_ref[r] = g[...]
    gathers = []
    for k in range(1, 8):
        to = (r + k) % 8
        cp = copy(g, pc_ref.at[r], ss_e.at[k], rs_e.at[r], to, c)
        gathers.append(cp)

    for p in range(4):
        for q in range(p + 1):
            total = jnp.zeros((16, B), F32)
            for l in range(4):
                total = total + jnp.where(16 * l + c == pv[q], g[p, l], 0.0)
            acand[4 * p + q] = total
    for m in LOWER:
        @pl.when(c != m)
        def _():
            copy(acand.at[m], ra.at[c], ss_b.at[m], rs_b.at[c], r, m).start()

        @pl.when(c == m)
        def _():
            ra[m] = acand[m]
    for cp in gathers:
        cp.start()
    member = c % 4 <= c // 4

    @pl.when(member)
    def _():
        for n in range(16):
            @pl.when(c != n)
            def _():
                copy(acand.at[0], ra.at[n], ss_b.at[0], rs_b.at[n], r, n).wait_recv()
        ab[r] = jnp.sum(ra[...], axis=0)
        for k in range(1, 8):
            to = (r + k) % 8
            copy(ab.at[r], ab.at[r], ss_c.at[k], rs_c.at[r], to, c).start()
        for k in range(1, 8):
            frm = (r + 8 - k) % 8
            copy(ab.at[r], ab.at[frm], ss_c.at[k], rs_c.at[frm], frm, c).wait_recv()
        af_ref[c] = ab[...]
        for k in range(1, 16):
            to = (c + k) % 16
            copy(ab, af_ref.at[c], ss_d.at[k], rs_d.at[c], r, to).start()

    z = c // 2
    o = (z - r // 2 + 8) % 8
    relay = c % 2 == r % 2
    right = (c + 2) % 16
    left = (c + 14) % 16
    twin = c + 1 - 2 * (c % 2)

    def hop(h, k, src, do_right, do_left):
        @pl.when(do_right)
        def _():
            copy(src, pr_ref.at[h, k], ss_f.at[h, k, 0], rs_f.at[h, k], r, right).start()

        @pl.when(do_left)
        def _():
            copy(src, pr_ref.at[h, k], ss_f.at[h, k, 1], rs_f.at[h, k], r, left).start()

        copy(src, pr_ref.at[h, k], ss_f.at[h, k, 2], rs_f.at[h, k], r, twin).start()

    def wait_pr(h, k):
        copy(g, pr_ref.at[h, k], ss_f.at[h, k, 2], rs_f.at[h, k], r, twin).wait_recv()

    for k in range(8):
        @pl.when(r != k)
        def _():
            copy(g, pc_ref.at[k], ss_e.at[0], rs_e.at[k], r, c).wait_recv()

    @pl.when(relay)
    def _():
        for h in range(2):
            oh = (o + 8 - 4 * h) % 8

            @pl.when(oh == 0)
            def _():
                pr_ref[h] = pc_ref[...]
        for step in range(12):
            for h in range(2):
                oh = (o + 8 - 4 * h) % 8
                far = jnp.where(oh <= 4, oh, 8 - oh)
                k = step - far

                @pl.when(jnp.logical_and(k >= 0, k < 8))
                def _():
                    @pl.when(oh != 0)
                    def _():
                        wait_pr(h, k)

                    hop(h, k, pr_ref.at[h, k], oh <= 3, jnp.logical_or(oh == 0, oh >= 6))

    @pl.when(jnp.logical_not(relay))
    def _():
        for k in range(8):
            for h in range(2):
                wait_pr(h, k)

    for m in LOWER:
        @pl.when(c != m)
        def _():
            copy(ab, af_ref.at[m], ss_d.at[0], rs_d.at[m], r, m).wait_recv()
            copy(acand.at[m], ra.at[c], ss_b.at[m], rs_b.at[c], r, m).wait_send()
    for cp in first:
        cp.wait_send()
    for cp in gathers:
        cp.wait_send()

    @pl.when(member)
    def _():
        for k in range(1, 8):
            copy(ab.at[r], ab.at[r], ss_c.at[k], rs_c.at[r], (r + k) % 8, c).wait_send()
        for k in range(1, 16):
            copy(ab, af_ref.at[c], ss_d.at[k], rs_d.at[c], r, (c + k) % 16).wait_send()

    @pl.when(relay)
    def _():
        for k in range(8):
            for h in range(2):
                oh = (o + 8 - 4 * h) % 8

                @pl.when(oh <= 3)
                def _():
                    copy(g, pr_ref.at[h, k], ss_f.at[h, k, 0], rs_f.at[h, k], r, right).wait_send()

                @pl.when(jnp.logical_or(oh == 0, oh >= 6))
                def _():
                    copy(g, pr_ref.at[h, k], ss_f.at[h, k, 1], rs_f.at[h, k], r, left).wait_send()

                copy(g, pr_ref.at[h, k], ss_f.at[h, k, 2], rs_f.at[h, k], r, twin).wait_send()


def gather(pv, cm, contrib, fd):
    dma = pltpu.SemaphoreType.DMA
    vm = pl.BlockSpec(memory_space=pltpu.VMEM)
    sm = pl.BlockSpec(memory_space=pltpu.SMEM)
    return pl.pallas_call(
        gather_kernel,
        out_shape=(
            jax.ShapeDtypeStruct((16, 8, 16, B), F32),
            jax.ShapeDtypeStruct((8, 4, 4, 16, B), F32),
            jax.ShapeDtypeStruct((2, 8, 4, 4, 16, B), F32),
        ),
        in_specs=[sm, sm, vm, vm],
        out_specs=(vm, vm, vm),
        scratch_shapes=[
            pltpu.VMEM((8, 72, 256), F32),
            pltpu.VMEM((8, 72, 256), F32),
            pltpu.VMEM((4, 4, 16, B), F32),
            pltpu.VMEM((16, 16, B), F32),
            pltpu.VMEM((16, 16, B), F32),
            pltpu.VMEM((8, 16, B), F32),
            dma((8,)), dma((8,)), dma((16,)), dma((16,)), dma((8,)), dma((8,)),
            dma((16,)), dma((16,)), dma((8,)), dma((8,)), dma((2, 8, 3)), dma((2, 8)),
        ],
        compiler_params=pltpu.CompilerParams(
            collective_id=0, has_side_effects=True, vmem_limit_bytes=40 << 20
        ),
        name="gather",
    )(pv, cm, contrib, fd)


def factor_block(w_ref, r_ref, out_ref):
    row = lax.broadcasted_iota(jnp.int32, (16, 8, B), 0) * 8 + lax.broadcasted_iota(
        jnp.int32, (16, 8, B), 1
    )
    col = lax.broadcasted_iota(jnp.int32, (16, 8, B), 2)
    r_ref[...] = jnp.where(row == col, 1.0, 0.0).astype(F32)
    for t in range(16):
        w = w_ref[t]
        v = r_ref[t]
        cols = [jnp.broadcast_to(w[:, 8 * t + k:8 * t + k + 1], (8, B)) for k in range(8)]
        a = [[None] * 8 for _ in range(8)]
        for k in range(8):
            for i in range(k, 8):
                a[i][k] = jnp.broadcast_to(cols[k][i:i + 1, :], (8, B))
        wr = [jnp.broadcast_to(w[i:i + 1, :], (8, B)) for i in range(8)]
        vr = [jnp.broadcast_to(v[i:i + 1, :], (8, B)) for i in range(8)]
        rs = [None] * 8
        l = [[None] * 8 for _ in range(8)]
        for k in range(8):
            rs[k] = lax.rsqrt(a[k][k])
            for i in range(k + 1, 8):
                l[i][k] = a[i][k] * rs[k]
            for j in range(k + 1, 8):
                for i in range(j, 8):
                    a[i][j] = a[i][j] - l[i][k] * l[j][k]
            wr[k] = wr[k] * rs[k]
            vr[k] = vr[k] * rs[k]
            for i in range(k + 1, 8):
                wr[i] = wr[i] - l[i][k] * wr[k]
                vr[i] = vr[i] - l[i][k] * vr[k]
        for k in range(8):
            out_ref[8 * t + k:8 * t + k + 1, :] = vr[k][0:1, :]
        if t < 15:
            for k in range(7, -1, -1):
                for i in range(k + 1, 8):
                    wr[k] = wr[k] - l[i][k] * wr[i]
                    vr[k] = vr[k] - l[i][k] * vr[i]
                wr[k] = wr[k] * rs[k]
                vr[k] = vr[k] * rs[k]
            for u in range(t + 1, 16):
                old = w_ref[u]
                new = old
                inv = r_ref[u]
                for k in range(8):
                    factor = jnp.broadcast_to(old[:, 8 * t + k:8 * t + k + 1], (8, B))
                    new = new - factor * wr[k]
                    inv = inv - factor * vr[k]
                w_ref[u] = new
                r_ref[u] = inv


def cholesky_kernel(a_ref, l_ref, w_ref, r_ref):
    l_ref[...] = a_ref[...]

    def body(p, carry):
        w_ref[...] = l_ref[p, p].reshape(16, 8, B)
        factor_block(w_ref, r_ref, l_ref.at[p, p])
        inv = l_ref[p, p]

        def column(i, carry):
            @pl.when(i > p)
            def _():
                l_ref[i, p] = dot(l_ref[i, p], inv, 1, 1)
            return carry

        lax.fori_loop(0, 4, column, 0)

        def update(ij, carry):
            i = ij // 4
            j = ij % 4

            @pl.when(jnp.logical_and(j > p, i >= j))
            def _():
                l_ref[i, j] = l_ref[i, j] - dot(l_ref[i, p], l_ref[j, p], 1, 1)
            return carry

        lax.fori_loop(0, 16, update, 0)
        return carry

    lax.fori_loop(0, 4, body, 0)


def cholesky(a):
    vm = pl.BlockSpec(memory_space=pltpu.VMEM)
    return pl.pallas_call(
        cholesky_kernel,
        out_shape=jax.ShapeDtypeStruct((4, 4, B, B), F32),
        in_specs=[vm],
        out_specs=vm,
        scratch_shapes=[pltpu.VMEM((16, 8, B), F32)] * 2,
        name="cholesky",
        cost_estimate=pl.CostEstimate(flops=200_000_000, bytes_accessed=100_000_000, transcendentals=0),
    )(a)


def finish_kernel(pv, cm, pos, con_ref, x_ref, fd_ref, l_ref, pc_ref, pr_ref, lf_ref, s_ref, lt):
    r = pos[0]
    c = pos[1]
    s = r // 4
    for p in range(4):
        for k in range(8):
            blk = pr_ref[k % 2, :, p, k // 2].reshape(B, B)
            if p >= 2:
                gone = jnp.logical_or(8 * k + r == pv[0], 8 * k + r == pv[1])
                blk = jnp.where(gone, 0.0, blk)
            lt[p, :, k * B:(k + 1) * B] = blk
        for l in range(4):
            blk = pc_ref[:, p, l].reshape(B, B)
            lt[p, :, 1024 + l * B:1024 + (l + 1) * B] = blk
    for p in range(4):
        acc = lt[p]
        for q in range(p):
            acc = acc - dot(l_ref[p, q], lt[q], 1, 0)
        lt[p] = dot(l_ref[p, p], acc, 1, 0)
        if p >= 2:
            for k in range(8):
                gone = jnp.logical_or(8 * k + r == pv[0], 8 * k + r == pv[1])

                @pl.when(gone)
                def _():
                    lt[p, :, k * B:(k + 1) * B] = jnp.zeros((B, B), F32)
    mine = lt[c // 4, pl.ds(pl.multiple_of((c % 4) * 32, 32), 32), 0:1024]
    lf_ref[...] = mine.T
    row = lax.broadcasted_iota(jnp.int32, (B, B), 0)
    col = lax.broadcasted_iota(jnp.int32, (B, B), 1)
    for k in range(8):
        m = k % 4
        low = lt[:, :, k * B:(k + 1) * B].reshape(512, B)
        upd = dot(low, lt[:, :, 1024:1536].reshape(512, 512), 0, 0)
        own = con_ref[pl.ds(pl.multiple_of((2 * m + s) * B, B), B), :]
        other = x_ref[m]
        row_gone = jnp.zeros((), jnp.bool_)
        for p in range(4):
            row_gone = jnp.logical_or(row_gone, 8 * k + r == pv[p])
        own_row = cm[s, 8 * m + r] == 8 * k + r
        other_row = cm[1 - s, 8 * m + r] == 8 * k + r
        for l in range(4):
            i = l % 2
            front_col = 16 * l + c
            gone = row_gone
            for p in range(4):
                gone = jnp.logical_or(gone, front_col == pv[p])
            own_here = jnp.logical_and(own_row, cm[s, 16 * i + c] == front_col)
            other_here = jnp.logical_and(other_row, cm[1 - s, 16 * i + c] == front_col)
            tile = jnp.where(own_here, own[:, i * B:(i + 1) * B], 0.0)
            tile = tile + jnp.where(other_here, other[:, i * B:(i + 1) * B], 0.0)
            dk = jnp.where(row == col, jnp.broadcast_to(fd_ref[k:k + 1, :], (B, B)), 0.0)
            tile = tile + jnp.where(8 * k + r == front_col, dk, 0.0)
            tile = tile - upd[:, l * B:(l + 1) * B]
            s_ref[k * B:(k + 1) * B, l * B:(l + 1) * B] = jnp.where(gone, 0.0, tile)


def finish(pv, cm, pos, contrib, other, fd, low, pc, pr):
    vm = pl.BlockSpec(memory_space=pltpu.VMEM)
    sm = pl.BlockSpec(memory_space=pltpu.SMEM)
    return pl.pallas_call(
        finish_kernel,
        out_shape=(
            jax.ShapeDtypeStruct((1024, 32), F32),
            jax.ShapeDtypeStruct((1024, 512), F32),
        ),
        in_specs=[sm, sm, sm] + [vm] * 6,
        out_specs=(vm, vm),
        scratch_shapes=[pltpu.VMEM((4, B, 1536), F32)],
        compiler_params=pltpu.CompilerParams(vmem_limit_bytes=40 << 20),
        name="finish",
        cost_estimate=pl.CostEstimate(flops=1_000_000_000, bytes_accessed=8_000_000, transcendentals=0),
    )(pv, cm, pos, contrib, other, fd, low, pc, pr)


def per_device(contrib, front_diag, child_map, pivots):
    r = lax.axis_index("row")
    c = lax.axis_index("col")
    fd = front_diag.reshape(8, B)
    af, pc, pr = gather(pivots, child_map, contrib, fd)
    halves = contrib.reshape(4, 2, B, 256)
    away = lax.dynamic_index_in_dim(halves, 1 - r // 4, 1, keepdims=False)
    away, af = lax.optimization_barrier((away, af))
    other = lax.ppermute(away, "row", [(i, i ^ 4) for i in range(8)])
    low = cholesky(af.reshape(4, 4, B, B))
    pos = jnp.stack([r, c]).astype(jnp.int32)
    return finish(pivots, child_map, pos, contrib, other, fd, low, pc, pr)


def solution(mesh):
    placed = (P(("front", "row"), "col"), P(("front", "row")), P("front", None), P("front"))
    return jax.shard_map(
        per_device,
        mesh=mesh,
        in_specs=placed,
        out_specs=(P(("front", "row"), "col"), P(("front", "row"), "col")),
        check_vma=False,
    )
```

```python
import jax
import jax.numpy as jnp
from jax import lax
from jax.experimental import pallas as pl
from jax.experimental.pallas import tpu as pltpu
from jax.sharding import PartitionSpec as P

F32 = jnp.float32
HIGHEST = lax.Precision.HIGHEST
MESH = pl.DeviceIdType.MESH
B = 128


def dot(a, b, ca, cb):
    return lax.dot_general(
        a, b, (((ca,), (cb,)), ((), ())), precision=HIGHEST, preferred_element_type=F32
    )


def factor_block(w_ref, r_ref, out_ref, tick):
    row = lax.broadcasted_iota(jnp.int32, (16, 8, B), 0) * 8 + lax.broadcasted_iota(
        jnp.int32, (16, 8, B), 1
    )
    col = lax.broadcasted_iota(jnp.int32, (16, 8, B), 2)
    r_ref[...] = jnp.where(row == col, 1.0, 0.0).astype(F32)
    for t in range(16):
        tick(t)
        w = w_ref[t]
        v = r_ref[t]
        cols = [jnp.broadcast_to(w[:, 8 * t + k:8 * t + k + 1], (8, B)) for k in range(8)]
        a = [[None] * 8 for _ in range(8)]
        for k in range(8):
            for i in range(k, 8):
                a[i][k] = jnp.broadcast_to(cols[k][i:i + 1, :], (8, B))
        wr = [jnp.broadcast_to(w[i:i + 1, :], (8, B)) for i in range(8)]
        vr = [jnp.broadcast_to(v[i:i + 1, :], (8, B)) for i in range(8)]
        rs = [None] * 8
        l = [[None] * 8 for _ in range(8)]
        for k in range(8):
            rs[k] = lax.rsqrt(a[k][k])
            for i in range(k + 1, 8):
                l[i][k] = a[i][k] * rs[k]
            for j in range(k + 1, 8):
                for i in range(j, 8):
                    a[i][j] = a[i][j] - l[i][k] * l[j][k]
            wr[k] = wr[k] * rs[k]
            vr[k] = vr[k] * rs[k]
            for i in range(k + 1, 8):
                wr[i] = wr[i] - l[i][k] * wr[k]
                vr[i] = vr[i] - l[i][k] * vr[k]
        for k in range(8):
            out_ref[8 * t + k:8 * t + k + 1, :] = vr[k][0:1, :]
        if t < 15:
            for k in range(7, -1, -1):
                for i in range(k + 1, 8):
                    wr[k] = wr[k] - l[i][k] * wr[i]
                    vr[k] = vr[k] - l[i][k] * vr[i]
                wr[k] = wr[k] * rs[k]
                vr[k] = vr[k] * rs[k]
            for u in range(t + 1, 16):
                old = w_ref[u]
                new = old
                inv = r_ref[u]
                for k in range(8):
                    factor = jnp.broadcast_to(old[:, 8 * t + k:8 * t + k + 1], (8, B))
                    new = new - factor * wr[k]
                    inv = inv - factor * vr[k]
                w_ref[u] = new
                r_ref[u] = inv


def factor_kernel(
    pv, cm, con_ref, fd_ref, l_ref, pc_ref, pr_ref, x_ref,
    cand, rsb, acand, za, af, w_ref, r_ref,
    ss_a, rs_a, ss_b, rs_b, ss_c, rs_c, ss_e, rs_e, ss_f, rs_f, ss_x, rs_x,
):
    f = lax.axis_index("front")
    r = lax.axis_index("row")
    c = lax.axis_index("col")
    s = r // 4
    d = r % 4

    def copy(src, dst, ssem, rsem, row, col):
        return pltpu.make_async_remote_copy(
            src_ref=src, dst_ref=dst, send_sem=ssem, recv_sem=rsem,
            device_id=(f, row, col), device_id_type=MESH,
        )

    barrier = pltpu.get_barrier_semaphore()
    for k in range(1, 8):
        pl.semaphore_signal(barrier, inc=1, device_id=(f, (r + k) % 8, c), device_id_type=MESH)
    for k in range(1, 16):
        pl.semaphore_signal(barrier, inc=1, device_id=(f, r, (c + k) % 16), device_id_type=MESH)

    cand[:, 0:8, :] = jnp.zeros((8, 8, 256), F32)
    for p in range(4):
        b = pv[p] % 32
        mine = jnp.logical_and(cm[s, b] == pv[p], b % 4 == d)
        rows = con_ref[pl.ds((b // 4) * B, B), :]
        rows = jnp.where(mine, rows, 0.0)
        cand[:, 8 + p * 16:24 + p * 16, :] = rows.reshape(8, 16, 256)
        line = fd_ref[pl.ds(pv[p] // 8, 1), :]
        line = jnp.where(pv[p] % 8 == r, line, 0.0)
        cand[:, p:p + 1, 0:B] = jnp.broadcast_to(line[None], (8, 1, B))
    rsb[r] = cand[r]

    pl.semaphore_wait(barrier, 22)

    def span(p):
        return pl.ds(0, 24) if p == 0 else pl.ds(8 + 16 * p, 16)

    def rs_copy(p, k):
        to = (r + k) % 8
        return copy(cand.at[to, span(p)], rsb.at[r, span(p)], ss_a.at[p, k], rs_a.at[p, r], to, c)

    for p in range(4):
        for k in range(1, 8):
            rs_copy(p, k).start()

    lane = lax.broadcasted_iota(jnp.int32, (16, B), 1)
    sub = lax.broadcasted_iota(jnp.int32, (16, B), 0)
    on_diag = lane == sub + 16 * r

    def z_copy(p, k):
        to = (c + k) % 16
        return copy(
            acand.at[p, pl.ds(0, p + 1)], za.at[p, c, pl.ds(0, p + 1)],
            ss_b.at[p, k], rs_b.at[p, c], r, to,
        )

    def stage_z(p):
        for k in range(1, 8):
            frm = (r + k) % 8
            copy(
                cand.at[frm, span(p)], rsb.at[frm, span(p)], ss_a.at[p, k], rs_a.at[p, frm], frm, c
            ).wait_recv()
        rows = [rsb[n, 8 + 16 * p:24 + 16 * p, :] for n in range(8)]
        sums = [
            (rows[4 * ch] + rows[4 * ch + 1]) + (rows[4 * ch + 2] + rows[4 * ch + 3])
            for ch in range(2)
        ]
        diag = jnp.sum(rsb[:, p:p + 1, 0:B], axis=0)
        dp = jnp.where(on_diag, jnp.broadcast_to(diag, (16, B)), 0.0)
        parts = []
        for l in range(4):
            i = l % 2
            total = jnp.where(16 * l + c == pv[p], dp, 0.0)
            for ch in range(2):
                here = cm[ch, 16 * i + c] == 16 * l + c
                total = total + jnp.where(here, sums[ch][:, i * B:(i + 1) * B], 0.0)
            pc_ref[r, p, l] = total
            parts.append(total)
        for q in range(p + 1):
            total = jnp.zeros((16, B), F32)
            for l in range(4):
                total = total + jnp.where(16 * l + c == pv[q], parts[l], 0.0)
            acand[p, q] = total
            za[p, c, q] = total
        for k in range(1, 16):
            z_copy(p, k).start()

    def y_copy(p, k):
        to = (r + k) % 8
        here = af.at[p, r, pl.ds(0, p + 1)]
        return copy(here, here, ss_c.at[p, k], rs_c.at[p, r], to, c)

    def stage_y(p):
        for k in range(1, 16):
            frm = (c + k) % 16
            copy(
                acand.at[p, pl.ds(0, p + 1)], za.at[p, frm, pl.ds(0, p + 1)],
                ss_b.at[p, k], rs_b.at[p, frm], r, frm,
            ).wait_recv()
        af[p, r, 0:p + 1] = jnp.sum(za[p, :, 0:p + 1], axis=0)
        for k in range(1, 8):
            y_copy(p, k).start()

    def stage_a(p):
        for k in range(1, 8):
            frm = (r + k) % 8
            there = af.at[p, frm, pl.ds(0, p + 1)]
            copy(there, there, ss_c.at[p, k], rs_c.at[p, frm], frm, c).wait_recv()

    def ring(step, way):
        origin = (r + (8 - step + 1 if way == 0 else step - 1)) % 8
        to = (r + (1 if way == 0 else 7)) % 8
        chunk = pc_ref.at[origin]
        return copy(chunk, chunk, ss_e.at[way, step], rs_e.at[origin], to, c)

    def ring_recv(origin):
        chunk = pc_ref.at[origin]
        copy(chunk, chunk, ss_e.at[0, 1], rs_e.at[origin], r, c).wait_recv()

    def stage_ring(step):
        if step > 1:
            ring_recv((r + 8 - step + 1) % 8)
            if step <= 4:
                ring_recv((r + step - 1) % 8)
        if step <= 4:
            ring(step, 0).start()
        if step <= 3:
            ring(step, 1).start()

    z = c // 2
    o = (z - r // 2 + 8) % 8
    relay = c % 2 == r % 2
    right = (c + 2) % 16
    left = (c + 14) % 16
    twin = c + 1 - 2 * (c % 2)

    def relay_copy(h, n, way):
        chunk = pr_ref.at[h, n]
        to = (right, left, twin)[way]
        return copy(chunk, chunk, ss_f.at[h, n, way], rs_f.at[h, n], r, to)

    def ways(h):
        oh = (o + 8 - 4 * h) % 8
        return oh, oh <= 3, jnp.logical_or(oh == 0, oh >= 6)

    def stage_relay(step):
        @pl.when(relay)
        def _():
            for h in range(2):
                oh, go_right, go_left = ways(h)
                j = step - jnp.where(oh <= 4, oh, 8 - oh)
                n = (r + jnp.where(j % 2 == 0, j // 2, 8 - (j + 1) // 2)) % 8

                @pl.when(jnp.logical_and(j >= 0, j < 8))
                def _():
                    @pl.when(oh == 0)
                    def _():
                        pr_ref[h, n] = pc_ref[n]

                    @pl.when(oh != 0)
                    def _():
                        relay_copy(h, n, 2).wait_recv()

                    @pl.when(go_right)
                    def _():
                        relay_copy(h, n, 0).start()

                    @pl.when(go_left)
                    def _():
                        relay_copy(h, n, 1).start()

                    relay_copy(h, n, 2).start()

    def x_copy(m):
        rows = pl.ds((2 * m + 1 - s) * B, B)
        return copy(con_ref.at[rows], x_ref.at[m], ss_x.at[m], rs_x.at[m], (r + 4) % 8, c)

    stage_z(0)
    stage_z(1)
    stage_z(2)
    stage_y(0)
    stage_z(3)
    stage_ring(1)
    stage_relay(0)
    stage_y(1)

    actions = {
        2: [lambda: stage_ring(2), lambda: stage_relay(1)],
        8: [lambda: stage_relay(2)],
        10: [lambda: stage_y(2)],
        11: [lambda: stage_ring(3)],
        13: [lambda: x_copy(0).start()],
        14: [lambda: stage_relay(3)],
        19: [lambda: x_copy(1).start()],
        20: [lambda: stage_ring(4), lambda: stage_relay(4)],
        25: [lambda: x_copy(2).start()],
        26: [lambda: stage_relay(5)],
        28: [lambda: stage_y(3)],
        29: [lambda: stage_ring(5)],
        31: [lambda: x_copy(3).start()],
        32: [lambda: stage_relay(6)],
        38: [lambda: stage_relay(7)],
        44: [lambda: stage_relay(8)],
        50: [lambda: stage_relay(9)],
        56: [lambda: stage_relay(10)],
        62: [lambda: stage_relay(11)],
    }

    def block(p, carry):
        for n in range(4):
            @pl.when(p == n)
            def _():
                stage_a(n)

        def left_block(q, carry):
            def minus(j, acc):
                return acc - dot(l_ref[p, j], l_ref[q, j], 1, 1)

            acc = lax.fori_loop(0, q, minus, af[p, :, q].reshape(B, B))
            l_ref[p, q] = dot(acc, l_ref[q, q], 1, 1)
            return carry

        lax.fori_loop(0, p, left_block, 0)

        def minus(j, acc):
            low = l_ref[p, j]
            return acc - dot(low, low, 1, 1)

        acc = lax.fori_loop(0, p, minus, af[p, :, p].reshape(B, B))
        w_ref[...] = acc.reshape(16, 8, B)

        def tick(t):
            for n in range(4):
                if 16 * n + t in actions:
                    @pl.when(p == n)
                    def _():
                        for act in actions[16 * n + t]:
                            act()

        factor_block(w_ref, r_ref, l_ref.at[p, p], tick)
        return carry

    lax.fori_loop(0, 4, block, 0)

    for m in range(4):
        x_copy(m).wait()

    @pl.when(jnp.logical_not(relay))
    def _():
        for h in range(2):
            for n in range(8):
                relay_copy(h, n, 2).wait_recv()

    @pl.when(relay)
    def _():
        for h in range(2):
            _, go_right, go_left = ways(h)
            for n in range(8):
                @pl.when(go_right)
                def _():
                    relay_copy(h, n, 0).wait_send()

                @pl.when(go_left)
                def _():
                    relay_copy(h, n, 1).wait_send()

                relay_copy(h, n, 2).wait_send()
    for step in range(1, 5):
        ring(step, 0).wait_send()
        if step <= 3:
            ring(step, 1).wait_send()
    for p in range(4):
        for k in range(1, 8):
            rs_copy(p, k).wait_send()
            y_copy(p, k).wait_send()
        for k in range(1, 16):
            z_copy(p, k).wait_send()


def factor(pv, cm, contrib, fd):
    dma = pltpu.SemaphoreType.DMA
    vm = pl.BlockSpec(memory_space=pltpu.VMEM)
    sm = pl.BlockSpec(memory_space=pltpu.SMEM)
    return pl.pallas_call(
        factor_kernel,
        out_shape=(
            jax.ShapeDtypeStruct((4, 4, B, B), F32),
            jax.ShapeDtypeStruct((8, 4, 4, 16, B), F32),
            jax.ShapeDtypeStruct((2, 8, 4, 4, 16, B), F32),
            jax.ShapeDtypeStruct((4, B, 256), F32),
        ),
        in_specs=[sm, sm, vm, vm],
        out_specs=(vm, vm, vm, vm),
        scratch_shapes=[
            pltpu.VMEM((8, 72, 256), F32),
            pltpu.VMEM((8, 72, 256), F32),
            pltpu.VMEM((4, 4, 16, B), F32),
            pltpu.VMEM((4, 16, 4, 16, B), F32),
            pltpu.VMEM((4, 8, 4, 16, B), F32),
            pltpu.VMEM((16, 8, B), F32),
            pltpu.VMEM((16, 8, B), F32),
            dma((4, 8)), dma((4, 8)), dma((4, 16)), dma((4, 16)), dma((4, 8)), dma((4, 8)),
            dma((2, 5)), dma((8,)), dma((2, 8, 3)), dma((2, 8)), dma((4,)), dma((4,)),
        ],
        compiler_params=pltpu.CompilerParams(
            collective_id=0, has_side_effects=True, vmem_limit_bytes=20 << 20
        ),
        name="factor",
        cost_estimate=pl.CostEstimate(flops=200_000_000, bytes_accessed=10_000_000, transcendentals=0),
    )(pv, cm, contrib, fd)


def finish_kernel(pv, cm, pos, con_ref, x_ref, fd_ref, l_ref, pc_ref, pr_ref, lf_ref, s_ref, lt):
    r = pos[0]
    c = pos[1]
    s = r // 4
    for p in range(4):
        for k in range(8):
            blk = pr_ref[k % 2, :, p, k // 2].reshape(B, B)
            if p >= 2:
                gone = jnp.logical_or(8 * k + r == pv[0], 8 * k + r == pv[1])
                blk = jnp.where(gone, 0.0, blk)
            lt[p, :, k * B:(k + 1) * B] = blk
        for l in range(4):
            blk = pc_ref[:, p, l].reshape(B, B)
            lt[p, :, 1024 + l * B:1024 + (l + 1) * B] = blk
    for p in range(4):
        acc = lt[p]
        for q in range(p):
            acc = acc - dot(l_ref[p, q], lt[q], 1, 0)
        lt[p] = dot(l_ref[p, p], acc, 1, 0)
        if p >= 2:
            for k in range(8):
                gone = jnp.logical_or(8 * k + r == pv[0], 8 * k + r == pv[1])

                @pl.when(gone)
                def _():
                    lt[p, :, k * B:(k + 1) * B] = jnp.zeros((B, B), F32)
    mine = lt[c // 4, pl.ds(pl.multiple_of((c % 4) * 32, 32), 32), 0:1024]
    lf_ref[...] = mine.T
    row = lax.broadcasted_iota(jnp.int32, (B, B), 0)
    col = lax.broadcasted_iota(jnp.int32, (B, B), 1)
    for k in range(8):
        m = k % 4
        low = lt[:, :, k * B:(k + 1) * B].reshape(512, B)
        upd = dot(low, lt[:, :, 1024:1536].reshape(512, 512), 0, 0)
        own = con_ref[pl.ds(pl.multiple_of((2 * m + s) * B, B), B), :]
        other = x_ref[m]
        row_gone = jnp.zeros((), jnp.bool_)
        for p in range(4):
            row_gone = jnp.logical_or(row_gone, 8 * k + r == pv[p])
        own_row = cm[s, 8 * m + r] == 8 * k + r
        other_row = cm[1 - s, 8 * m + r] == 8 * k + r
        for l in range(4):
            i = l % 2
            front_col = 16 * l + c
            gone = row_gone
            for p in range(4):
                gone = jnp.logical_or(gone, front_col == pv[p])
            own_here = jnp.logical_and(own_row, cm[s, 16 * i + c] == front_col)
            other_here = jnp.logical_and(other_row, cm[1 - s, 16 * i + c] == front_col)
            tile = jnp.where(own_here, own[:, i * B:(i + 1) * B], 0.0)
            tile = tile + jnp.where(other_here, other[:, i * B:(i + 1) * B], 0.0)
            dk = jnp.where(row == col, jnp.broadcast_to(fd_ref[k:k + 1, :], (B, B)), 0.0)
            tile = tile + jnp.where(8 * k + r == front_col, dk, 0.0)
            tile = tile - upd[:, l * B:(l + 1) * B]
            s_ref[k * B:(k + 1) * B, l * B:(l + 1) * B] = jnp.where(gone, 0.0, tile)


def finish(pv, cm, pos, contrib, other, fd, low, pc, pr):
    vm = pl.BlockSpec(memory_space=pltpu.VMEM)
    sm = pl.BlockSpec(memory_space=pltpu.SMEM)
    return pl.pallas_call(
        finish_kernel,
        out_shape=(
            jax.ShapeDtypeStruct((1024, 32), F32),
            jax.ShapeDtypeStruct((1024, 512), F32),
        ),
        in_specs=[sm, sm, sm] + [vm] * 6,
        out_specs=(vm, vm),
        scratch_shapes=[pltpu.VMEM((4, B, 1536), F32)],
        compiler_params=pltpu.CompilerParams(vmem_limit_bytes=24 << 20),
        name="finish",
        cost_estimate=pl.CostEstimate(flops=1_000_000_000, bytes_accessed=8_000_000, transcendentals=0),
    )(pv, cm, pos, contrib, other, fd, low, pc, pr)


def per_device(contrib, front_diag, child_map, pivots):
    r = lax.axis_index("row")
    c = lax.axis_index("col")
    fd = front_diag.reshape(8, B)
    low, pc, pr, other = factor(pivots, child_map, contrib, fd)
    pos = jnp.stack([r, c]).astype(jnp.int32)
    return finish(pivots, child_map, pos, contrib, other, fd, low, pc, pr)


def solution(mesh):
    placed = (P(("front", "row"), "col"), P(("front", "row")), P("front", None), P("front"))
    return jax.shard_map(
        per_device,
        mesh=mesh,
        in_specs=placed,
        out_specs=(P(("front", "row"), "col"), P(("front", "row"), "col")),
        check_vma=False,
    )
```

```python
import jax
import jax.numpy as jnp
from jax import lax
from jax.experimental import pallas as pl
from jax.experimental.pallas import tpu as pltpu
from jax.sharding import PartitionSpec as P

F32 = jnp.float32
HIGHEST = lax.Precision.HIGHEST
MESH = pl.DeviceIdType.MESH
B = 128


def dot(a, b, ca, cb):
    return lax.dot_general(
        a, b, (((ca,), (cb,)), ((), ())), precision=HIGHEST, preferred_element_type=F32
    )


def split(x):
    high = x.astype(jnp.bfloat16)
    return high, (x - high.astype(F32)).astype(jnp.bfloat16)


def bdot(a, b):
    return lax.dot_general(a, b, (((1,), (0,)), ((), ())), preferred_element_type=F32)


def fetch(*pairs, sem):
    copies = [pltpu.make_async_copy(src, dst, sem.at[n]) for n, (src, dst) in enumerate(pairs)]
    for cp in copies:
        cp.start()
    return copies


def factor_block(w_ref, r_ref, out_ref, tick):
    row = lax.broadcasted_iota(jnp.int32, (16, 8, B), 0) * 8 + lax.broadcasted_iota(
        jnp.int32, (16, 8, B), 1
    )
    col = lax.broadcasted_iota(jnp.int32, (16, 8, B), 2)
    r_ref[...] = jnp.where(row == col, 1.0, 0.0).astype(F32)
    for t in range(16):
        tick(t)
        w = w_ref[t]
        v = r_ref[t]
        cols = [jnp.broadcast_to(w[:, 8 * t + k:8 * t + k + 1], (8, B)) for k in range(8)]
        a = [[None] * 8 for _ in range(8)]
        for k in range(8):
            for i in range(k, 8):
                a[i][k] = jnp.broadcast_to(cols[k][i:i + 1, :], (8, B))
        wr = [jnp.broadcast_to(w[i:i + 1, :], (8, B)) for i in range(8)]
        vr = [jnp.broadcast_to(v[i:i + 1, :], (8, B)) for i in range(8)]
        rs = [None] * 8
        l = [[None] * 8 for _ in range(8)]
        for k in range(8):
            rs[k] = lax.rsqrt(a[k][k])
            for i in range(k + 1, 8):
                l[i][k] = a[i][k] * rs[k]
            for j in range(k + 1, 8):
                for i in range(j, 8):
                    a[i][j] = a[i][j] - l[i][k] * l[j][k]
            wr[k] = wr[k] * rs[k]
            vr[k] = vr[k] * rs[k]
            for i in range(k + 1, 8):
                wr[i] = wr[i] - l[i][k] * wr[k]
                vr[i] = vr[i] - l[i][k] * vr[k]
        for k in range(8):
            out_ref[8 * t + k:8 * t + k + 1, :] = vr[k][0:1, :]
        if t < 15:
            for k in range(7, -1, -1):
                for i in range(k + 1, 8):
                    wr[k] = wr[k] - l[i][k] * wr[i]
                    vr[k] = vr[k] - l[i][k] * vr[i]
                wr[k] = wr[k] * rs[k]
                vr[k] = vr[k] * rs[k]
            for u in range(t + 1, 16):
                old = w_ref[u]
                new = old
                inv = r_ref[u]
                for k in range(8):
                    factor = jnp.broadcast_to(old[:, 8 * t + k:8 * t + k + 1], (8, B))
                    new = new - factor * wr[k]
                    inv = inv - factor * vr[k]
                w_ref[u] = new
                r_ref[u] = inv


def number(p, q):
    return p * (p + 1) // 2 + q


def home(p, q):
    return (number(p, q) - 1) * 2 % 16 + (number(p, q) - 1) // 8


def factor_kernel(
    pv_any, cm_any, con_any, fd_any, lf_any, s_any,
    l_ref, pc_ref, pr_ref, x_ref, lt, rows_hi, rows_lo, cols_hi, cols_lo, lf, st, out_sem, pv, cm, con_ref, fd_ref, sem, cand, rsb, acand, za, zb, ab, af, w_ref, r_ref,
    ss_a, rs_a, ss_z, rs_z, ss_b, rs_b, ss_g, rs_g, ss_h, ss_c, rs_c, ss_w, rs_w, ss_e, rs_e, ss_o, ss_p, rs_p, ss_t, ss_x, rs_x,
):
    f = lax.axis_index("front")
    r = lax.axis_index("row")
    c = lax.axis_index("col")
    s = r // 4
    d = r % 4

    def copy(src, dst, ssem, rsem, row, col):
        return pltpu.make_async_remote_copy(
            src_ref=src, dst_ref=dst, send_sem=ssem, recv_sem=rsem,
            device_id=(f, row, col), device_id_type=MESH,
        )

    fetches = fetch(
        (pv_any, pv), (cm_any, cm), (fd_any, fd_ref), (con_any, con_ref), sem=sem
    )
    barrier = pltpu.get_barrier_semaphore()
    for k in range(1, 8):
        pl.semaphore_signal(barrier, inc=1, device_id=(f, (r + k) % 8, c), device_id_type=MESH)
    for k in range(1, 16):
        pl.semaphore_signal(barrier, inc=1, device_id=(f, r, (c + k) % 16), device_id_type=MESH)
    out_row, out_col = c % 8, 2 * r + c // 8
    in_row, in_col = c // 2, r + 8 * (c % 2)
    stays = jnp.logical_and(out_row == r, out_col == c)

    @pl.when(jnp.logical_not(stays))
    def _():
        pl.semaphore_signal(barrier, inc=1, device_id=(f, out_row, out_col), device_id_type=MESH)
        pl.semaphore_signal(barrier, inc=1, device_id=(f, in_row, in_col), device_id_type=MESH)

    cand[:, 0:8, :] = jnp.zeros((8, 8, 256), F32)
    for cp in fetches:
        cp.wait()
    for p in range(4):
        b = pv[p] % 32
        mine = jnp.logical_and(cm[s, b] == pv[p], b % 4 == d)
        rows = con_ref[pl.ds((b // 4) * B, B), :]
        rows = jnp.where(mine, rows, 0.0)
        cand[:, 8 + p * 16:24 + p * 16, :] = rows.reshape(8, 16, 256)
        line = fd_ref[pl.ds(pv[p] // 8, 1), :]
        line = jnp.where(pv[p] % 8 == r, line, 0.0)
        cand[:, p:p + 1, 0:B] = jnp.broadcast_to(line[None], (8, 1, B))
    rsb[r] = cand[r]

    pl.semaphore_wait(barrier, jnp.where(stays, 22, 24))

    def span(p):
        return pl.ds(0, 24) if p == 0 else pl.ds(8 + 16 * p, 16)

    def rs_copy(p, k):
        to = (r + k) % 8
        return copy(cand.at[to, span(p)], rsb.at[r, span(p)], ss_a.at[p, k], rs_a.at[p, r], to, c)

    for p in range(4):
        for k in range(1, 8):
            rs_copy(p, k).start()

    lane = lax.broadcasted_iota(jnp.int32, (16, B), 1)
    sub = lax.broadcasted_iota(jnp.int32, (16, B), 0)
    on_diag = lane == sub + 16 * r

    def z_copy(k):
        to = (c + k) % 16
        return copy(acand.at[0, 0], za.at[c], ss_z.at[k], rs_z.at[c], r, to)

    def b_copy(p, q):
        return copy(acand.at[p, q], zb.at[c], ss_b.at[p, q], rs_b.at[c], r, home(p, q))

    def y_copy(k):
        return copy(ab.at[r], ab.at[r], ss_c.at[k], rs_c.at[r], (r + k) % 8, c)

    def g_copy(p, q, k):
        return copy(ab, af.at[number(p, q)], ss_g.at[k], rs_g.at[p, q], r, (c + 2 * k) % 16)

    def h_copy(p, q):
        block = af.at[number(p, q)]
        return copy(block, block, ss_h.at[p, q], rs_g.at[p, q], r, c + 1 - 2 * (c % 2))

    def forwards(p, q):
        return jnp.logical_and(c % 2 == home(p, q) % 2, c != home(p, q))

    def stage_t(p):
        for q in range(p + 1):
            @pl.when(forwards(p, q))
            def _():
                copy(ab, af.at[number(p, q)], ss_g.at[1], rs_g.at[p, q], r, c).wait_recv()
                h_copy(p, q).start()

    def stage_z(p):
        for k in range(1, 8):
            frm = (r + k) % 8
            copy(
                cand.at[frm, span(p)], rsb.at[frm, span(p)], ss_a.at[p, k], rs_a.at[p, frm], frm, c
            ).wait_recv()
        rows = [rsb[n, 8 + 16 * p:24 + 16 * p, :] for n in range(8)]
        sums = [
            (rows[4 * ch] + rows[4 * ch + 1]) + (rows[4 * ch + 2] + rows[4 * ch + 3])
            for ch in range(2)
        ]
        diag = jnp.sum(rsb[:, p:p + 1, 0:B], axis=0)
        dp = jnp.where(on_diag, jnp.broadcast_to(diag, (16, B)), 0.0)
        parts = []
        for l in range(4):
            i = l % 2
            total = jnp.where(16 * l + c == pv[p], dp, 0.0)
            for ch in range(2):
                here = cm[ch, 16 * i + c] == 16 * l + c
                total = total + jnp.where(here, sums[ch][:, i * B:(i + 1) * B], 0.0)
            pc_ref[r, p, l] = total
            parts.append(total)
        for q in range(p + 1):
            total = jnp.zeros((16, B), F32)
            for l in range(4):
                total = total + jnp.where(16 * l + c == pv[q], parts[l], 0.0)
            acand[p, q] = total
        if p == 0:
            za[c] = acand[0, 0]
            for k in range(1, 16):
                z_copy(k).start()
        else:
            for q in range(p + 1):
                @pl.when(c != home(p, q))
                def _():
                    b_copy(p, q).start()

                @pl.when(c == home(p, q))
                def _():
                    zb[c] = acand[p, q]

    def stage_m(p):
        for q in range(p + 1):
            @pl.when(c == home(p, q))
            def _():
                for k in range(1, 16):
                    frm = (c + k) % 16
                    copy(acand.at[p, q], zb.at[frm], ss_b.at[p, q], rs_b.at[frm], r, frm).wait_recv()
                ab[r] = jnp.sum(zb[...], axis=0)
                for k in range(1, 8):
                    y_copy(k).start()

    def wait_ab():
        for k in range(1, 8):
            frm = (r + k) % 8
            copy(ab.at[frm], ab.at[frm], ss_c.at[k], rs_c.at[frm], frm, c).wait_recv()

    def stage_y(p):
        if p == 0:
            for k in range(1, 16):
                frm = (c + k) % 16
                copy(acand.at[0, 0], za.at[frm], ss_z.at[k], rs_z.at[frm], r, frm).wait_recv()
            af[0, r] = jnp.sum(za[...], axis=0)
            for k in range(1, 8):
                w_copy(k).start()
        else:
            for q in range(p + 1):
                @pl.when(c == home(p, q))
                def _():
                    wait_ab()
                    for k in range(1, 8):
                        g_copy(p, q, k).start()
                    af[number(p, q)] = ab[...]
                    h_copy(p, q).start()

    def w_copy(k):
        return copy(af.at[0, r], af.at[0, r], ss_w.at[k], rs_w.at[r], (r + k) % 8, c)

    def stage_a(p):
        if p == 0:
            for k in range(1, 8):
                frm = (r + k) % 8
                copy(af.at[0, frm], af.at[0, frm], ss_w.at[k], rs_w.at[frm], frm, c).wait_recv()
        else:
            for q in range(p + 1):
                @pl.when(c % 2 != home(p, q) % 2)
                def _():
                    copy(ab, af.at[number(p, q)], ss_g.at[1], rs_g.at[p, q], r, c).wait_recv()

    def ring(step, way):
        origin = (r + (8 - step + 1 if way == 0 else step - 1)) % 8
        to = (r + (1 if way == 0 else 7)) % 8
        chunk = pc_ref.at[origin]
        return copy(chunk, chunk, ss_e.at[way, step], rs_e.at[origin], to, c)

    def ring_recv(origin):
        chunk = pc_ref.at[origin]
        copy(chunk, chunk, ss_e.at[0, 1], rs_e.at[origin], r, c).wait_recv()

    def stage_ring(step):
        if step > 1:
            ring_recv((r + 8 - step + 1) % 8)
            if step <= 4:
                ring_recv((r + step - 1) % 8)
        if step <= 4:
            ring(step, 0).start()
        if step <= 3:
            ring(step, 1).start()

    chip = c // 2
    core = c % 2

    def out_copy():
        return copy(pc_ref.at[r], pr_ref.at[out_col], ss_o.at[0], rs_p.at[out_col], out_row, out_col)

    def share_recv(n):
        copy(pc_ref.at[0], pr_ref.at[n], ss_o.at[0], rs_p.at[n], r, c).wait_recv()

    def z_ring(step, way):
        n = 2 * ((chip + (8 - step + 1 if way == 0 else step - 1)) % 8) + core
        to = (c + (2 if way == 0 else 14)) % 16
        return copy(pr_ref.at[n], pr_ref.at[n], ss_p.at[way, step], rs_p.at[n], r, to)

    def twin_copy(k):
        n = 2 * ((chip + k) % 8) + core
        return copy(pr_ref.at[n], pr_ref.at[n], ss_t.at[k], rs_p.at[n], r, c + 1 - 2 * core)

    def stage_out():
        @pl.when(stays)
        def _():
            pr_ref[c] = pc_ref[r]

        @pl.when(jnp.logical_not(stays))
        def _():
            out_copy().start()

    def stage_share(step):
        if step == 1:
            @pl.when(jnp.logical_not(stays))
            def _():
                share_recv(c)
            twin_copy(0).start()
        else:
            share_recv(2 * ((chip + 8 - step + 1) % 8) + core)
            twin_copy(8 - step + 1).start()
            if step <= 4:
                share_recv(2 * ((chip + step - 1) % 8) + core)
                twin_copy(step - 1).start()
        if step <= 4:
            z_ring(step, 0).start()
        if step <= 3:
            z_ring(step, 1).start()

    def x_copy(m):
        rows = pl.ds((2 * m + 1 - s) * B, B)
        return copy(con_ref.at[rows], x_ref.at[m], ss_x.at[m], rs_x.at[m], (r + 4) % 8, c)

    stage_z(0)
    stage_z(1)
    stage_z(2)
    stage_y(0)
    stage_z(3)
    stage_m(1)
    stage_m(2)
    stage_m(3)
    stage_out()

    actions = {
        0: [lambda: stage_y(1)],
        1: [lambda: stage_y(2)],
        2: [lambda: stage_y(3), lambda: stage_ring(1)],
        6: [lambda: x_copy(0).start()],
        8: [lambda: stage_share(1)],
        10: [lambda: stage_t(1)],
        12: [lambda: stage_ring(2)],
        13: [lambda: x_copy(1).start()],
        17: [lambda: stage_share(2), lambda: stage_t(2)],
        21: [lambda: stage_ring(3)],
        22: [lambda: x_copy(2).start()],
        23: [lambda: stage_t(3)],
        26: [lambda: stage_share(3)],
        30: [lambda: stage_ring(4)],
        31: [lambda: x_copy(3).start()],
        35: [lambda: stage_share(4)],
        39: [lambda: stage_ring(5)],
        43: [lambda: stage_share(5)],
    }

    def block(p, carry):
        for n in range(4):
            @pl.when(p == n)
            def _():
                stage_a(n)

        def left_block(q, carry):
            def minus(j, acc):
                return acc - dot(l_ref[p, j], l_ref[q, j], 1, 1)

            acc = lax.fori_loop(0, q, minus, af[number(p, q)].reshape(B, B))
            l_ref[p, q] = dot(acc, l_ref[q, q], 1, 1)
            return carry

        lax.fori_loop(0, p, left_block, 0)

        def minus(j, acc):
            low = l_ref[p, j]
            return acc - dot(low, low, 1, 1)

        acc = lax.fori_loop(0, p, minus, af[number(p, p)].reshape(B, B))
        w_ref[...] = acc.reshape(16, 8, B)

        def tick(t):
            for n in range(4):
                if 16 * n + t in actions:
                    @pl.when(p == n)
                    def _():
                        for act in actions[16 * n + t]:
                            act()

        factor_block(w_ref, r_ref, l_ref.at[p, p], tick)
        return carry

    lax.fori_loop(0, 4, block, 0)

    for k in range(8):
        share_recv(2 * k + 1 - core)
    for p in range(4):
        for k in range(8):
            lt[p, :, k * B:(k + 1) * B] = jnp.concatenate([pr_ref[2 * n + k % 2, p, k // 2] for n in range(8)], axis=0)
        for l in range(4):
            lt[p, :, 1024 + l * B:1024 + (l + 1) * B] = pc_ref[:, p, l].reshape(B, B)
    for p in range(4):
        acc = lt[p]
        if p > 0:
            low = jnp.concatenate([l_ref[p, q] for q in range(p)], axis=1)
            acc = acc - dot(low, lt[0:p].reshape(p * B, 1536), 1, 0)
        lt[p] = dot(l_ref[p, p], acc, 1, 0)
        if p >= 2:
            for k in range(8):
                gone = jnp.logical_or(8 * k + r == pv[0], 8 * k + r == pv[1])
                kept = lt[p, :, k * B:(k + 1) * B]
                lt[p, :, k * B:(k + 1) * B] = jnp.where(gone, 0.0, kept)
        hi, lo = split(lt[p])
        rows_hi[:, p * B:(p + 1) * B] = hi[:, 0:1024].T
        rows_lo[:, p * B:(p + 1) * B] = lo[:, 0:1024].T
        cols_hi[p * B:(p + 1) * B, :] = hi[:, 1024:1536]
        cols_lo[p * B:(p + 1) * B, :] = lo[:, 1024:1536]
    lf[...] = lt[c // 4, pl.ds(pl.multiple_of((c % 4) * 32, 32), 32), 0:1024]
    lf_copy = pltpu.make_async_copy(lf, lf_any, out_sem.at[2])
    lf_copy.start()
    for m in range(4):
        x_copy(m).wait()
    row = lax.broadcasted_iota(jnp.int32, (B, B), 0)
    col = lax.broadcasted_iota(jnp.int32, (B, B), 1)
    stores = []
    for half in range(2):
        part = slice(half * 512, (half + 1) * 512)
        st[part, :] = (
            bdot(rows_hi[part, :], cols_hi[...])
            + (bdot(rows_hi[part, :], cols_lo[...]) + bdot(rows_lo[part, :], cols_hi[...]))
        )
        for m in range(4):
            k = 4 * half + m
            own = con_ref[pl.ds(pl.multiple_of((2 * m + s) * B, B), B), :]
            other = x_ref[m]
            row_gone = 8 * k + r == pv[0]
            for p in range(1, 4):
                row_gone = jnp.logical_or(row_gone, 8 * k + r == pv[p])
            own_row = cm[s, 8 * m + r] == 8 * k + r
            other_row = cm[1 - s, 8 * m + r] == 8 * k + r
            dk = jnp.where(row == col, jnp.broadcast_to(fd_ref[k:k + 1, :], (B, B)), 0.0)
            for l in range(4):
                i = l % 2
                front_col = 16 * l + c
                gone = row_gone
                for p in range(4):
                    gone = jnp.logical_or(gone, front_col == pv[p])
                own_here = jnp.logical_and(own_row, cm[s, 16 * i + c] == front_col)
                other_here = jnp.logical_and(other_row, cm[1 - s, 16 * i + c] == front_col)
                tile = jnp.where(own_here, own[:, i * B:(i + 1) * B], 0.0)
                tile = tile + jnp.where(other_here, other[:, i * B:(i + 1) * B], 0.0)
                tile = tile + jnp.where(8 * k + r == front_col, dk, 0.0)
                at = (slice(k * B, (k + 1) * B), slice(l * B, (l + 1) * B))
                st[at] = jnp.where(gone, 0.0, tile - st[at])
        store = pltpu.make_async_copy(
            st.at[pl.ds(half * 512, 512)], s_any.at[pl.ds(half * 512, 512)], out_sem.at[half]
        )
        store.start()
        stores.append(store)
    for k in range(8):
        twin_copy(k).wait_send()

    @pl.when(jnp.logical_not(stays))
    def _():
        out_copy().wait_send()
    for step in range(1, 5):
        ring(step, 0).wait_send()
        z_ring(step, 0).wait_send()
        if step <= 3:
            ring(step, 1).wait_send()
            z_ring(step, 1).wait_send()
    for p in range(4):
        for k in range(1, 8):
            rs_copy(p, k).wait_send()
    for k in range(1, 8):
        w_copy(k).wait_send()
    for k in range(1, 16):
        z_copy(k).wait_send()
    for p in range(1, 4):
        for q in range(p + 1):
            @pl.when(c != home(p, q))
            def _():
                b_copy(p, q).wait_send()

            @pl.when(c == home(p, q))
            def _():
                for k in range(1, 8):
                    y_copy(k).wait_send()
                for k in range(1, 8):
                    g_copy(p, q, k).wait_send()

            @pl.when(c % 2 == home(p, q) % 2)
            def _():
                h_copy(p, q).wait_send()
    for store in stores:
        store.wait()
    lf_copy.wait()


def factor(pv, cm, contrib, fd):
    dma = pltpu.SemaphoreType.DMA
    hbm = pl.BlockSpec(memory_space=pltpu.HBM)
    return pl.pallas_call(
        factor_kernel,
        out_shape=(
            jax.ShapeDtypeStruct((32, 1024), F32),
            jax.ShapeDtypeStruct((1024, 512), F32),
        ),
        in_specs=[hbm] * 4,
        out_specs=(hbm, hbm),
        scratch_shapes=[
            pltpu.VMEM((4, 4, B, B), F32),
            pltpu.VMEM((8, 4, 4, 16, B), F32),
            pltpu.VMEM((16, 4, 4, 16, B), F32),
            pltpu.VMEM((4, B, 256), F32),
            pltpu.VMEM((4, B, 1536), F32),
            pltpu.VMEM((1024, 512), jnp.bfloat16),
            pltpu.VMEM((1024, 512), jnp.bfloat16),
            pltpu.VMEM((512, 512), jnp.bfloat16),
            pltpu.VMEM((512, 512), jnp.bfloat16),
            pltpu.VMEM((32, 1024), F32),
            pltpu.VMEM((1024, 512), F32),
            dma((3,)),
            pltpu.SMEM((4,), jnp.int32),
            pltpu.SMEM((2, 32), jnp.int32),
            pltpu.VMEM((1024, 256), F32),
            pltpu.VMEM((8, B), F32),
            dma((4,)),
            pltpu.VMEM((8, 72, 256), F32),
            pltpu.VMEM((8, 72, 256), F32),
            pltpu.VMEM((4, 4, 16, B), F32),
            pltpu.VMEM((16, 16, B), F32),
            pltpu.VMEM((16, 16, B), F32),
            pltpu.VMEM((8, 16, B), F32),
            pltpu.VMEM((10, 8, 16, B), F32),
            pltpu.VMEM((16, 8, B), F32),
            pltpu.VMEM((16, 8, B), F32),
            dma((4, 8)), dma((4, 8)), dma((16,)), dma((16,)), dma((4, 4)), dma((16,)),
            dma((16,)), dma((4, 4)), dma((4, 4)), dma((8,)), dma((8,)), dma((8,)), dma((8,)),
            dma((2, 5)), dma((8,)), dma((1,)), dma((2, 5)), dma((16,)), dma((8,)), dma((4,)), dma((4,)),
        ],
        compiler_params=pltpu.CompilerParams(
            collective_id=0, has_side_effects=True, vmem_limit_bytes=60 << 20
        ),
        name="factor",
        cost_estimate=pl.CostEstimate(flops=200_000_000, bytes_accessed=10_000_000, transcendentals=0),
    )(pv, cm, contrib, fd)


def per_device(contrib, front_diag, child_map, pivots):
    fd = front_diag.reshape(8, B)
    lf, schur = factor(pivots, child_map, contrib, fd)
    return lf.T, schur


def solution(mesh):
    placed = (P(("front", "row"), "col"), P(("front", "row")), P("front", None), P("front"))
    return jax.shard_map(
        per_device,
        mesh=mesh,
        in_specs=placed,
        out_specs=(P(("front", "row"), "col"), P(("front", "row"), "col")),
        check_vma=False,
    )
```

```python
import jax
import jax.numpy as jnp
from jax import lax
from jax.experimental import pallas as pl
from jax.experimental.pallas import tpu as pltpu
from jax.sharding import PartitionSpec as P

F32 = jnp.float32
HIGHEST = lax.Precision.HIGHEST
MESH = pl.DeviceIdType.MESH
B = 128


def dot(a, b, ca, cb):
    return lax.dot_general(
        a, b, (((ca,), (cb,)), ((), ())), precision=HIGHEST, preferred_element_type=F32
    )


def split(x):
    high = x.astype(jnp.bfloat16)
    return high, (x - high.astype(F32)).astype(jnp.bfloat16)


def bdot(a, b):
    return lax.dot_general(a, b, (((1,), (0,)), ((), ())), preferred_element_type=F32)


def fetch(*pairs, sem):
    copies = [pltpu.make_async_copy(src, dst, sem.at[n]) for n, (src, dst) in enumerate(pairs)]
    for cp in copies:
        cp.start()
    return copies


def factor_block(w_ref, r_ref, out_ref, tick):
    row = lax.broadcasted_iota(jnp.int32, (16, 8, B), 0) * 8 + lax.broadcasted_iota(
        jnp.int32, (16, 8, B), 1
    )
    col = lax.broadcasted_iota(jnp.int32, (16, 8, B), 2)
    r_ref[...] = jnp.where(row == col, 1.0, 0.0).astype(F32)
    for t in range(16):
        tick(t)
        w = w_ref[t]
        v = r_ref[t]
        cols = [jnp.broadcast_to(w[:, 8 * t + k:8 * t + k + 1], (8, B)) for k in range(8)]
        a = [[None] * 8 for _ in range(8)]
        for k in range(8):
            for i in range(k, 8):
                a[i][k] = jnp.broadcast_to(cols[k][i:i + 1, :], (8, B))
        wr = [jnp.broadcast_to(w[i:i + 1, :], (8, B)) for i in range(8)]
        vr = [jnp.broadcast_to(v[i:i + 1, :], (8, B)) for i in range(8)]
        rs = [None] * 8
        l = [[None] * 8 for _ in range(8)]
        for k in range(8):
            rs[k] = lax.rsqrt(a[k][k])
            for i in range(k + 1, 8):
                l[i][k] = a[i][k] * rs[k]
            for j in range(k + 1, 8):
                for i in range(j, 8):
                    a[i][j] = a[i][j] - l[i][k] * l[j][k]
            wr[k] = wr[k] * rs[k]
            vr[k] = vr[k] * rs[k]
            for i in range(k + 1, 8):
                wr[i] = wr[i] - l[i][k] * wr[k]
                vr[i] = vr[i] - l[i][k] * vr[k]
        for k in range(8):
            out_ref[8 * t + k:8 * t + k + 1, :] = vr[k][0:1, :]
        if t < 15:
            for k in range(7, -1, -1):
                for i in range(k + 1, 8):
                    wr[k] = wr[k] - l[i][k] * wr[i]
                    vr[k] = vr[k] - l[i][k] * vr[i]
                wr[k] = wr[k] * rs[k]
                vr[k] = vr[k] * rs[k]
            for u in range(t + 1, 16):
                old = w_ref[u]
                new = old
                inv = r_ref[u]
                for k in range(8):
                    factor = jnp.broadcast_to(old[:, 8 * t + k:8 * t + k + 1], (8, B))
                    new = new - factor * wr[k]
                    inv = inv - factor * vr[k]
                w_ref[u] = new
                r_ref[u] = inv


def number(p, q):
    return p * (p + 1) // 2 + q


def home(p, q):
    return (number(p, q) - 1) * 2 % 16 + (number(p, q) - 1) // 8


def factor_kernel(
    pv_any, cm_any, con_any, fd_any, lf, st,
    l_ref, pc_ref, pr_ref, x_ref, lt, rows_hi, rows_lo, cols_hi, cols_lo, pv, cm, con_ref, fd_ref, sem, cand, rsb, acand, za, zb, ab, af, w_ref, r_ref,
    ss_a, rs_a, ss_z, rs_z, ss_b, rs_b, ss_g, rs_g, ss_h, ss_c, rs_c, ss_w, rs_w, ss_e, rs_e, ss_o, ss_p, rs_p, ss_t, ss_x, rs_x,
):
    f = lax.axis_index("front")
    r = lax.axis_index("row")
    c = lax.axis_index("col")
    s = r // 4
    d = r % 4

    def copy(src, dst, ssem, rsem, row, col):
        return pltpu.make_async_remote_copy(
            src_ref=src, dst_ref=dst, send_sem=ssem, recv_sem=rsem,
            device_id=(f, row, col), device_id_type=MESH,
        )

    fetches = fetch(
        (pv_any, pv), (cm_any, cm), (fd_any, fd_ref), (con_any, con_ref), sem=sem
    )
    barrier = pltpu.get_barrier_semaphore()
    for k in range(1, 8):
        pl.semaphore_signal(barrier, inc=1, device_id=(f, (r + k) % 8, c), device_id_type=MESH)
    for k in range(1, 16):
        pl.semaphore_signal(barrier, inc=1, device_id=(f, r, (c + k) % 16), device_id_type=MESH)
    out_row, out_col = c % 8, 2 * r + c // 8
    in_row, in_col = c // 2, r + 8 * (c % 2)
    stays = jnp.logical_and(out_row == r, out_col == c)

    @pl.when(jnp.logical_not(stays))
    def _():
        pl.semaphore_signal(barrier, inc=1, device_id=(f, out_row, out_col), device_id_type=MESH)
        pl.semaphore_signal(barrier, inc=1, device_id=(f, in_row, in_col), device_id_type=MESH)

    cand[:, 0:8, :] = jnp.zeros((8, 8, 256), F32)
    for cp in fetches:
        cp.wait()
    for p in range(4):
        b = pv[p] % 32
        mine = jnp.logical_and(cm[s, b] == pv[p], b % 4 == d)
        rows = con_ref[pl.ds((b // 4) * B, B), :]
        rows = jnp.where(mine, rows, 0.0)
        cand[:, 8 + p * 16:24 + p * 16, :] = rows.reshape(8, 16, 256)
        line = fd_ref[pl.ds(pv[p] // 8, 1), :]
        line = jnp.where(pv[p] % 8 == r, line, 0.0)
        cand[:, p:p + 1, 0:B] = jnp.broadcast_to(line[None], (8, 1, B))
    rsb[r] = cand[r]

    pl.semaphore_wait(barrier, jnp.where(stays, 22, 24))

    def span(p):
        return pl.ds(0, 24) if p == 0 else pl.ds(8 + 16 * p, 16)

    def rs_copy(p, k):
        to = (r + k) % 8
        return copy(cand.at[to, span(p)], rsb.at[r, span(p)], ss_a.at[p, k], rs_a.at[p, r], to, c)

    for p in range(4):
        for k in range(1, 8):
            rs_copy(p, k).start()

    lane = lax.broadcasted_iota(jnp.int32, (16, B), 1)
    sub = lax.broadcasted_iota(jnp.int32, (16, B), 0)
    on_diag = lane == sub + 16 * r

    def z_copy(k):
        to = (c + k) % 16
        return copy(acand.at[0, 0], za.at[c], ss_z.at[k], rs_z.at[c], r, to)

    def b_copy(p, q):
        return copy(acand.at[p, q], zb.at[c], ss_b.at[p, q], rs_b.at[c], r, home(p, q))

    def y_copy(k):
        return copy(ab.at[r], ab.at[r], ss_c.at[k], rs_c.at[r], (r + k) % 8, c)

    def g_copy(p, q, k):
        return copy(ab, af.at[number(p, q)], ss_g.at[k], rs_g.at[p, q], r, (c + 2 * k) % 16)

    def h_copy(p, q):
        block = af.at[number(p, q)]
        return copy(block, block, ss_h.at[p, q], rs_g.at[p, q], r, c + 1 - 2 * (c % 2))

    def forwards(p, q):
        return jnp.logical_and(c % 2 == home(p, q) % 2, c != home(p, q))

    def stage_t(p):
        for q in range(p + 1):
            @pl.when(forwards(p, q))
            def _():
                copy(ab, af.at[number(p, q)], ss_g.at[1], rs_g.at[p, q], r, c).wait_recv()
                h_copy(p, q).start()

    def stage_z(p):
        for k in range(1, 8):
            frm = (r + k) % 8
            copy(
                cand.at[frm, span(p)], rsb.at[frm, span(p)], ss_a.at[p, k], rs_a.at[p, frm], frm, c
            ).wait_recv()
        rows = [rsb[n, 8 + 16 * p:24 + 16 * p, :] for n in range(8)]
        sums = [
            (rows[4 * ch] + rows[4 * ch + 1]) + (rows[4 * ch + 2] + rows[4 * ch + 3])
            for ch in range(2)
        ]
        diag = jnp.sum(rsb[:, p:p + 1, 0:B], axis=0)
        dp = jnp.where(on_diag, jnp.broadcast_to(diag, (16, B)), 0.0)
        parts = []
        for l in range(4):
            i = l % 2
            total = jnp.where(16 * l + c == pv[p], dp, 0.0)
            for ch in range(2):
                here = cm[ch, 16 * i + c] == 16 * l + c
                total = total + jnp.where(here, sums[ch][:, i * B:(i + 1) * B], 0.0)
            pc_ref[r, p, l] = total
            parts.append(total)
        for q in range(p + 1):
            total = jnp.zeros((16, B), F32)
            for l in range(4):
                total = total + jnp.where(16 * l + c == pv[q], parts[l], 0.0)
            acand[p, q] = total
        if p == 0:
            za[c] = acand[0, 0]
            for k in range(1, 16):
                z_copy(k).start()
        else:
            for q in range(p + 1):
                @pl.when(c != home(p, q))
                def _():
                    b_copy(p, q).start()

                @pl.when(c == home(p, q))
                def _():
                    zb[c] = acand[p, q]

    def stage_m(p):
        for q in range(p + 1):
            @pl.when(c == home(p, q))
            def _():
                for k in range(1, 16):
                    frm = (c + k) % 16
                    copy(acand.at[p, q], zb.at[frm], ss_b.at[p, q], rs_b.at[frm], r, frm).wait_recv()
                ab[r] = jnp.sum(zb[...], axis=0)
                for k in range(1, 8):
                    y_copy(k).start()

    def wait_ab():
        for k in range(1, 8):
            frm = (r + k) % 8
            copy(ab.at[frm], ab.at[frm], ss_c.at[k], rs_c.at[frm], frm, c).wait_recv()

    def stage_y(p):
        if p == 0:
            for k in range(1, 16):
                frm = (c + k) % 16
                copy(acand.at[0, 0], za.at[frm], ss_z.at[k], rs_z.at[frm], r, frm).wait_recv()
            af[0, r] = jnp.sum(za[...], axis=0)
            for k in range(1, 8):
                w_copy(k).start()
        else:
            for q in range(p + 1):
                @pl.when(c == home(p, q))
                def _():
                    wait_ab()
                    for k in range(1, 8):
                        g_copy(p, q, k).start()
                    af[number(p, q)] = ab[...]
                    h_copy(p, q).start()

    def w_copy(k):
        return copy(af.at[0, r], af.at[0, r], ss_w.at[k], rs_w.at[r], (r + k) % 8, c)

    def stage_a(p):
        if p == 0:
            for k in range(1, 8):
                frm = (r + k) % 8
                copy(af.at[0, frm], af.at[0, frm], ss_w.at[k], rs_w.at[frm], frm, c).wait_recv()
        else:
            for q in range(p + 1):
                @pl.when(c % 2 != home(p, q) % 2)
                def _():
                    copy(ab, af.at[number(p, q)], ss_g.at[1], rs_g.at[p, q], r, c).wait_recv()

    def ring(step, way):
        origin = (r + (8 - step + 1 if way == 0 else step - 1)) % 8
        to = (r + (1 if way == 0 else 7)) % 8
        chunk = pc_ref.at[origin]
        return copy(chunk, chunk, ss_e.at[way, step], rs_e.at[origin], to, c)

    def ring_recv(origin):
        chunk = pc_ref.at[origin]
        copy(chunk, chunk, ss_e.at[0, 1], rs_e.at[origin], r, c).wait_recv()

    def stage_ring(step):
        if step > 1:
            ring_recv((r + 8 - step + 1) % 8)
            if step <= 4:
                ring_recv((r + step - 1) % 8)
        if step <= 4:
            ring(step, 0).start()
        if step <= 3:
            ring(step, 1).start()

    chip = c // 2
    core = c % 2

    def out_copy():
        return copy(pc_ref.at[r], pr_ref.at[out_col], ss_o.at[0], rs_p.at[out_col], out_row, out_col)

    def share_recv(n):
        copy(pc_ref.at[0], pr_ref.at[n], ss_o.at[0], rs_p.at[n], r, c).wait_recv()

    def z_ring(step, way):
        n = 2 * ((chip + (8 - step + 1 if way == 0 else step - 1)) % 8) + core
        to = (c + (2 if way == 0 else 14)) % 16
        return copy(pr_ref.at[n], pr_ref.at[n], ss_p.at[way, step], rs_p.at[n], r, to)

    def twin_copy(k):
        n = 2 * ((chip + k) % 8) + core
        return copy(pr_ref.at[n], pr_ref.at[n], ss_t.at[k], rs_p.at[n], r, c + 1 - 2 * core)

    def stage_out():
        @pl.when(stays)
        def _():
            pr_ref[c] = pc_ref[r]

        @pl.when(jnp.logical_not(stays))
        def _():
            out_copy().start()

    def stage_share(step):
        if step == 1:
            @pl.when(jnp.logical_not(stays))
            def _():
                share_recv(c)
            twin_copy(0).start()
        else:
            share_recv(2 * ((chip + 8 - step + 1) % 8) + core)
            twin_copy(8 - step + 1).start()
            if step <= 4:
                share_recv(2 * ((chip + step - 1) % 8) + core)
                twin_copy(step - 1).start()
        if step <= 4:
            z_ring(step, 0).start()
        if step <= 3:
            z_ring(step, 1).start()

    def x_copy(m):
        rows = pl.ds((2 * m + 1 - s) * B, B)
        return copy(con_ref.at[rows], x_ref.at[m], ss_x.at[m], rs_x.at[m], (r + 4) % 8, c)

    stage_z(0)
    stage_z(1)
    stage_z(2)
    stage_y(0)
    stage_z(3)
    stage_m(1)
    stage_m(2)
    stage_m(3)
    stage_out()

    actions = {
        0: [lambda: stage_y(1)],
        1: [lambda: stage_y(2)],
        2: [lambda: stage_y(3), lambda: stage_ring(1)],
        6: [lambda: x_copy(0).start()],
        8: [lambda: stage_share(1)],
        10: [lambda: stage_t(1)],
        12: [lambda: stage_ring(2)],
        13: [lambda: x_copy(1).start()],
        17: [lambda: stage_share(2), lambda: stage_t(2)],
        21: [lambda: stage_ring(3)],
        22: [lambda: x_copy(2).start()],
        23: [lambda: stage_t(3)],
        26: [lambda: stage_share(3)],
        30: [lambda: stage_ring(4)],
        31: [lambda: x_copy(3).start()],
        35: [lambda: stage_share(4)],
        39: [lambda: stage_ring(5)],
        43: [lambda: stage_share(5)],
    }

    def block(p, carry):
        for n in range(4):
            @pl.when(p == n)
            def _():
                stage_a(n)

        def left_block(q, carry):
            def minus(j, acc):
                return acc - dot(l_ref[p, j], l_ref[q, j], 1, 1)

            acc = lax.fori_loop(0, q, minus, af[number(p, q)].reshape(B, B))
            l_ref[p, q] = dot(acc, l_ref[q, q], 1, 1)
            return carry

        lax.fori_loop(0, p, left_block, 0)

        def minus(j, acc):
            low = l_ref[p, j]
            return acc - dot(low, low, 1, 1)

        acc = lax.fori_loop(0, p, minus, af[number(p, p)].reshape(B, B))
        w_ref[...] = acc.reshape(16, 8, B)

        def tick(t):
            for n in range(4):
                if 16 * n + t in actions:
                    @pl.when(p == n)
                    def _():
                        for act in actions[16 * n + t]:
                            act()

        factor_block(w_ref, r_ref, l_ref.at[p, p], tick)
        return carry

    lax.fori_loop(0, 4, block, 0)

    for k in range(8):
        share_recv(2 * k + 1 - core)
    for p in range(4):
        for k in range(8):
            lt[p, :, k * B:(k + 1) * B] = jnp.concatenate([pr_ref[2 * n + k % 2, p, k // 2] for n in range(8)], axis=0)
        for l in range(4):
            lt[p, :, 1024 + l * B:1024 + (l + 1) * B] = pc_ref[:, p, l].reshape(B, B)
    for p in range(4):
        acc = lt[p]
        if p > 0:
            low = jnp.concatenate([l_ref[p, q] for q in range(p)], axis=1)
            acc = acc - dot(low, lt[0:p].reshape(p * B, 1536), 1, 0)
        lt[p] = dot(l_ref[p, p], acc, 1, 0)
        if p >= 2:
            for k in range(8):
                gone = jnp.logical_or(8 * k + r == pv[0], 8 * k + r == pv[1])
                kept = lt[p, :, k * B:(k + 1) * B]
                lt[p, :, k * B:(k + 1) * B] = jnp.where(gone, 0.0, kept)
        hi, lo = split(lt[p])
        rows_hi[:, p * B:(p + 1) * B] = hi[:, 0:1024].T
        rows_lo[:, p * B:(p + 1) * B] = lo[:, 0:1024].T
        cols_hi[p * B:(p + 1) * B, :] = hi[:, 1024:1536]
        cols_lo[p * B:(p + 1) * B, :] = lo[:, 1024:1536]
    lf[...] = lt[c // 4, pl.ds(pl.multiple_of((c % 4) * 32, 32), 32), 0:1024]
    for m in range(4):
        x_copy(m).wait()
    row = lax.broadcasted_iota(jnp.int32, (B, B), 0)
    col = lax.broadcasted_iota(jnp.int32, (B, B), 1)
    for half in range(2):
        part = slice(half * 512, (half + 1) * 512)
        st[part, :] = (
            bdot(rows_hi[part, :], cols_hi[...])
            + (bdot(rows_hi[part, :], cols_lo[...]) + bdot(rows_lo[part, :], cols_hi[...]))
        )
        for m in range(4):
            k = 4 * half + m
            own = con_ref[pl.ds(pl.multiple_of((2 * m + s) * B, B), B), :]
            other = x_ref[m]
            row_gone = 8 * k + r == pv[0]
            for p in range(1, 4):
                row_gone = jnp.logical_or(row_gone, 8 * k + r == pv[p])
            own_row = cm[s, 8 * m + r] == 8 * k + r
            other_row = cm[1 - s, 8 * m + r] == 8 * k + r
            dk = jnp.where(row == col, jnp.broadcast_to(fd_ref[k:k + 1, :], (B, B)), 0.0)
            for l in range(4):
                i = l % 2
                front_col = 16 * l + c
                gone = row_gone
                for p in range(4):
                    gone = jnp.logical_or(gone, front_col == pv[p])
                own_here = jnp.logical_and(own_row, cm[s, 16 * i + c] == front_col)
                other_here = jnp.logical_and(other_row, cm[1 - s, 16 * i + c] == front_col)
                tile = jnp.where(own_here, own[:, i * B:(i + 1) * B], 0.0)
                tile = tile + jnp.where(other_here, other[:, i * B:(i + 1) * B], 0.0)
                tile = tile + jnp.where(8 * k + r == front_col, dk, 0.0)
                at = (slice(k * B, (k + 1) * B), slice(l * B, (l + 1) * B))
                st[at] = jnp.where(gone, 0.0, tile - st[at])
    for k in range(8):
        twin_copy(k).wait_send()

    @pl.when(jnp.logical_not(stays))
    def _():
        out_copy().wait_send()
    for step in range(1, 5):
        ring(step, 0).wait_send()
        z_ring(step, 0).wait_send()
        if step <= 3:
            ring(step, 1).wait_send()
            z_ring(step, 1).wait_send()
    for p in range(4):
        for k in range(1, 8):
            rs_copy(p, k).wait_send()
    for k in range(1, 8):
        w_copy(k).wait_send()
    for k in range(1, 16):
        z_copy(k).wait_send()
    for p in range(1, 4):
        for q in range(p + 1):
            @pl.when(c != home(p, q))
            def _():
                b_copy(p, q).wait_send()

            @pl.when(c == home(p, q))
            def _():
                for k in range(1, 8):
                    y_copy(k).wait_send()
                for k in range(1, 8):
                    g_copy(p, q, k).wait_send()

            @pl.when(c % 2 == home(p, q) % 2)
            def _():
                h_copy(p, q).wait_send()


def factor(pv, cm, contrib, fd):
    dma = pltpu.SemaphoreType.DMA
    hbm = pl.BlockSpec(memory_space=pltpu.HBM)
    vm = pl.BlockSpec(memory_space=pltpu.VMEM)
    return pl.pallas_call(
        factor_kernel,
        out_shape=(
            jax.ShapeDtypeStruct((32, 1024), F32),
            jax.ShapeDtypeStruct((1024, 512), F32),
        ),
        in_specs=[hbm] * 4,
        out_specs=(vm, vm),
        scratch_shapes=[
            pltpu.VMEM((4, 4, B, B), F32),
            pltpu.VMEM((8, 4, 4, 16, B), F32),
            pltpu.VMEM((16, 4, 4, 16, B), F32),
            pltpu.VMEM((4, B, 256), F32),
            pltpu.VMEM((4, B, 1536), F32),
            pltpu.VMEM((1024, 512), jnp.bfloat16),
            pltpu.VMEM((1024, 512), jnp.bfloat16),
            pltpu.VMEM((512, 512), jnp.bfloat16),
            pltpu.VMEM((512, 512), jnp.bfloat16),
            pltpu.SMEM((4,), jnp.int32),
            pltpu.SMEM((2, 32), jnp.int32),
            pltpu.VMEM((1024, 256), F32),
            pltpu.VMEM((8, B), F32),
            dma((4,)),
            pltpu.VMEM((8, 72, 256), F32),
            pltpu.VMEM((8, 72, 256), F32),
            pltpu.VMEM((4, 4, 16, B), F32),
            pltpu.VMEM((16, 16, B), F32),
            pltpu.VMEM((16, 16, B), F32),
            pltpu.VMEM((8, 16, B), F32),
            pltpu.VMEM((10, 8, 16, B), F32),
            pltpu.VMEM((16, 8, B), F32),
            pltpu.VMEM((16, 8, B), F32),
            dma((4, 8)), dma((4, 8)), dma((16,)), dma((16,)), dma((4, 4)), dma((16,)),
            dma((16,)), dma((4, 4)), dma((4, 4)), dma((8,)), dma((8,)), dma((8,)), dma((8,)),
            dma((2, 5)), dma((8,)), dma((1,)), dma((2, 5)), dma((16,)), dma((8,)), dma((4,)), dma((4,)),
        ],
        compiler_params=pltpu.CompilerParams(
            collective_id=0, has_side_effects=True, vmem_limit_bytes=60 << 20
        ),
        name="factor",
        cost_estimate=pl.CostEstimate(flops=200_000_000, bytes_accessed=10_000_000, transcendentals=0),
    )(pv, cm, contrib, fd)


def per_device(contrib, front_diag, child_map, pivots):
    fd = front_diag.reshape(8, B)
    lf, schur = factor(pivots, child_map, contrib, fd)
    return lf.T, schur


def solution(mesh):
    placed = (P(("front", "row"), "col"), P(("front", "row")), P("front", None), P("front"))
    return jax.shard_map(
        per_device,
        mesh=mesh,
        in_specs=placed,
        out_specs=(P(("front", "row"), "col"), P(("front", "row"), "col")),
        check_vma=False,
    )
```

```python
import jax
import jax.numpy as jnp
from jax import lax
from jax.experimental import pallas as pl
from jax.experimental.pallas import tpu as pltpu
from jax.sharding import PartitionSpec as P

F32 = jnp.float32
HIGHEST = lax.Precision.HIGHEST
MESH = pl.DeviceIdType.MESH
B = 128


def dot(a, b, ca, cb):
    return lax.dot_general(
        a, b, (((ca,), (cb,)), ((), ())), precision=HIGHEST, preferred_element_type=F32
    )


def split(x):
    high = x.astype(jnp.bfloat16)
    return high, (x - high.astype(F32)).astype(jnp.bfloat16)


def bdot(a, b):
    return lax.dot_general(a, b, (((1,), (0,)), ((), ())), preferred_element_type=F32)


def fetch(*pairs, sem):
    copies = [pltpu.make_async_copy(src, dst, sem.at[n]) for n, (src, dst) in enumerate(pairs)]
    for cp in copies:
        cp.start()
    return copies


def factor_block(w_ref, r_ref, out_ref, tick):
    row = lax.broadcasted_iota(jnp.int32, (16, 8, B), 0) * 8 + lax.broadcasted_iota(
        jnp.int32, (16, 8, B), 1
    )
    col = lax.broadcasted_iota(jnp.int32, (16, 8, B), 2)
    r_ref[...] = jnp.where(row == col, 1.0, 0.0).astype(F32)
    for t in range(16):
        tick(t)
        w = w_ref[t]
        v = r_ref[t]
        cols = [jnp.broadcast_to(w[:, 8 * t + k:8 * t + k + 1], (8, B)) for k in range(8)]
        a = [[None] * 8 for _ in range(8)]
        for k in range(8):
            for i in range(k, 8):
                a[i][k] = jnp.broadcast_to(cols[k][i:i + 1, :], (8, B))
        wr = [jnp.broadcast_to(w[i:i + 1, :], (8, B)) for i in range(8)]
        vr = [jnp.broadcast_to(v[i:i + 1, :], (8, B)) for i in range(8)]
        rs = [None] * 8
        l = [[None] * 8 for _ in range(8)]
        for k in range(8):
            rs[k] = lax.rsqrt(a[k][k])
            for i in range(k + 1, 8):
                l[i][k] = a[i][k] * rs[k]
            for j in range(k + 1, 8):
                for i in range(j, 8):
                    a[i][j] = a[i][j] - l[i][k] * l[j][k]
            wr[k] = wr[k] * rs[k]
            vr[k] = vr[k] * rs[k]
            for i in range(k + 1, 8):
                wr[i] = wr[i] - l[i][k] * wr[k]
                vr[i] = vr[i] - l[i][k] * vr[k]
        for k in range(8):
            out_ref[8 * t + k:8 * t + k + 1, :] = vr[k][0:1, :]
        if t < 15:
            for k in range(7, -1, -1):
                for i in range(k + 1, 8):
                    wr[k] = wr[k] - l[i][k] * wr[i]
                    vr[k] = vr[k] - l[i][k] * vr[i]
                wr[k] = wr[k] * rs[k]
                vr[k] = vr[k] * rs[k]
            for u in range(t + 1, 16):
                old = w_ref[u]
                new = old
                inv = r_ref[u]
                for k in range(8):
                    factor = jnp.broadcast_to(old[:, 8 * t + k:8 * t + k + 1], (8, B))
                    new = new - factor * wr[k]
                    inv = inv - factor * vr[k]
                w_ref[u] = new
                r_ref[u] = inv


def number(p, q):
    return p * (p + 1) // 2 + q


def home(p, q):
    return (number(p, q) - 1) * 2 % 16 + (number(p, q) - 1) // 8


def factor_kernel(
    pv_any, cm_any, con_any, fd_any, lf_any, s_any,
    l_ref, pc_ref, pr_ref, x_ref, lt, rows_hi, rows_lo, cols_hi, cols_lo, lf, st, out_sem, pv, cm, con_ref, fd_ref, sem, cand, rsb, acand, za, zb, ab, af, w_ref, r_ref,
    ss_a, rs_a, ss_z, rs_z, ss_b, rs_b, ss_g, rs_g, ss_h, ss_c, rs_c, ss_w, rs_w, ss_e, rs_e, ss_o, ss_p, rs_p, ss_t, ss_x, rs_x,
):
    f = lax.axis_index("front")
    r = lax.axis_index("row")
    c = lax.axis_index("col")
    s = r // 4
    d = r % 4

    def copy(src, dst, ssem, rsem, row, col):
        return pltpu.make_async_remote_copy(
            src_ref=src, dst_ref=dst, send_sem=ssem, recv_sem=rsem,
            device_id=(f, row, col), device_id_type=MESH,
        )

    fetches = fetch(
        (pv_any, pv), (cm_any, cm), (fd_any, fd_ref), (con_any, con_ref), sem=sem
    )
    barrier = pltpu.get_barrier_semaphore()
    for k in range(1, 8):
        pl.semaphore_signal(barrier, inc=1, device_id=(f, (r + k) % 8, c), device_id_type=MESH)
    for k in range(1, 16):
        pl.semaphore_signal(barrier, inc=1, device_id=(f, r, (c + k) % 16), device_id_type=MESH)
    out_row, out_col = c % 8, 2 * r + c // 8
    in_row, in_col = c // 2, r + 8 * (c % 2)
    stays = jnp.logical_and(out_row == r, out_col == c)

    @pl.when(jnp.logical_not(stays))
    def _():
        pl.semaphore_signal(barrier, inc=1, device_id=(f, out_row, out_col), device_id_type=MESH)
        pl.semaphore_signal(barrier, inc=1, device_id=(f, in_row, in_col), device_id_type=MESH)

    cand[:, 0:8, :] = jnp.zeros((8, 8, 256), F32)
    for cp in fetches:
        cp.wait()
    for p in range(4):
        b = pv[p] % 32
        mine = jnp.logical_and(cm[s, b] == pv[p], b % 4 == d)
        rows = con_ref[pl.ds((b // 4) * B, B), :]
        rows = jnp.where(mine, rows, 0.0)
        cand[:, 8 + p * 16:24 + p * 16, :] = rows.reshape(8, 16, 256)
        line = fd_ref[pl.ds(pv[p] // 8, 1), :]
        line = jnp.where(pv[p] % 8 == r, line, 0.0)
        cand[:, p:p + 1, 0:B] = jnp.broadcast_to(line[None], (8, 1, B))
    rsb[r] = cand[r]

    pl.semaphore_wait(barrier, jnp.where(stays, 22, 24))

    def span(p):
        return pl.ds(0, 24) if p == 0 else pl.ds(8 + 16 * p, 16)

    def rs_copy(p, k):
        to = (r + k) % 8
        return copy(cand.at[to, span(p)], rsb.at[r, span(p)], ss_a.at[p, k], rs_a.at[p, r], to, c)

    for p in range(4):
        for k in range(1, 8):
            rs_copy(p, k).start()

    lane = lax.broadcasted_iota(jnp.int32, (16, B), 1)
    sub = lax.broadcasted_iota(jnp.int32, (16, B), 0)
    on_diag = lane == sub + 16 * r

    def z_copy(k):
        to = (c + k) % 16
        return copy(acand.at[0, 0], za.at[c], ss_z.at[k], rs_z.at[c], r, to)

    def b_copy(p, q):
        return copy(acand.at[p, q], zb.at[c], ss_b.at[p, q], rs_b.at[c], r, home(p, q))

    def y_copy(k):
        return copy(ab.at[r], ab.at[r], ss_c.at[k], rs_c.at[r], (r + k) % 8, c)

    def g_copy(p, q, k):
        return copy(ab, af.at[number(p, q)], ss_g.at[k], rs_g.at[p, q], r, (c + 2 * k) % 16)

    def h_copy(p, q):
        block = af.at[number(p, q)]
        return copy(block, block, ss_h.at[p, q], rs_g.at[p, q], r, c + 1 - 2 * (c % 2))

    def forwards(p, q):
        return jnp.logical_and(c % 2 == home(p, q) % 2, c != home(p, q))

    def stage_t(p):
        for q in range(p + 1):
            @pl.when(forwards(p, q))
            def _():
                copy(ab, af.at[number(p, q)], ss_g.at[1], rs_g.at[p, q], r, c).wait_recv()
                h_copy(p, q).start()

    def stage_z(p):
        for k in range(1, 8):
            frm = (r + k) % 8
            copy(
                cand.at[frm, span(p)], rsb.at[frm, span(p)], ss_a.at[p, k], rs_a.at[p, frm], frm, c
            ).wait_recv()
        rows = [rsb[n, 8 + 16 * p:24 + 16 * p, :] for n in range(8)]
        sums = [
            (rows[4 * ch] + rows[4 * ch + 1]) + (rows[4 * ch + 2] + rows[4 * ch + 3])
            for ch in range(2)
        ]
        diag = jnp.sum(rsb[:, p:p + 1, 0:B], axis=0)
        dp = jnp.where(on_diag, jnp.broadcast_to(diag, (16, B)), 0.0)
        parts = []
        for l in range(4):
            i = l % 2
            total = jnp.where(16 * l + c == pv[p], dp, 0.0)
            for ch in range(2):
                here = cm[ch, 16 * i + c] == 16 * l + c
                total = total + jnp.where(here, sums[ch][:, i * B:(i + 1) * B], 0.0)
            pc_ref[r, p, l] = total
            parts.append(total)
        for q in range(p + 1):
            total = jnp.zeros((16, B), F32)
            for l in range(4):
                total = total + jnp.where(16 * l + c == pv[q], parts[l], 0.0)
            acand[p, q] = total
        if p == 0:
            za[c] = acand[0, 0]
            for k in range(1, 16):
                z_copy(k).start()
        else:
            for q in range(p + 1):
                @pl.when(c != home(p, q))
                def _():
                    b_copy(p, q).start()

                @pl.when(c == home(p, q))
                def _():
                    zb[c] = acand[p, q]

    def stage_m(p):
        for q in range(p + 1):
            @pl.when(c == home(p, q))
            def _():
                for k in range(1, 16):
                    frm = (c + k) % 16
                    copy(acand.at[p, q], zb.at[frm], ss_b.at[p, q], rs_b.at[frm], r, frm).wait_recv()
                ab[r] = jnp.sum(zb[...], axis=0)
                for k in range(1, 8):
                    y_copy(k).start()

    def wait_ab():
        for k in range(1, 8):
            frm = (r + k) % 8
            copy(ab.at[frm], ab.at[frm], ss_c.at[k], rs_c.at[frm], frm, c).wait_recv()

    def stage_y(p):
        if p == 0:
            for k in range(1, 16):
                frm = (c + k) % 16
                copy(acand.at[0, 0], za.at[frm], ss_z.at[k], rs_z.at[frm], r, frm).wait_recv()
            af[0, r] = jnp.sum(za[...], axis=0)
            for k in range(1, 8):
                w_copy(k).start()
        else:
            for q in range(p + 1):
                @pl.when(c == home(p, q))
                def _():
                    wait_ab()
                    for k in range(1, 8):
                        g_copy(p, q, k).start()
                    af[number(p, q)] = ab[...]
                    h_copy(p, q).start()

    def w_copy(k):
        return copy(af.at[0, r], af.at[0, r], ss_w.at[k], rs_w.at[r], (r + k) % 8, c)

    def stage_a(p):
        if p == 0:
            for k in range(1, 8):
                frm = (r + k) % 8
                copy(af.at[0, frm], af.at[0, frm], ss_w.at[k], rs_w.at[frm], frm, c).wait_recv()
        else:
            for q in range(p + 1):
                @pl.when(c % 2 != home(p, q) % 2)
                def _():
                    copy(ab, af.at[number(p, q)], ss_g.at[1], rs_g.at[p, q], r, c).wait_recv()

    def ring(step, way):
        origin = (r + (8 - step + 1 if way == 0 else step - 1)) % 8
        to = (r + (1 if way == 0 else 7)) % 8
        chunk = pc_ref.at[origin]
        return copy(chunk, chunk, ss_e.at[way, step], rs_e.at[origin], to, c)

    def ring_recv(origin):
        chunk = pc_ref.at[origin]
        copy(chunk, chunk, ss_e.at[0, 1], rs_e.at[origin], r, c).wait_recv()

    def stage_ring(step):
        if step > 1:
            ring_recv((r + 8 - step + 1) % 8)
            if step <= 4:
                ring_recv((r + step - 1) % 8)
        if step <= 4:
            ring(step, 0).start()
        if step <= 3:
            ring(step, 1).start()

    chip = c // 2
    core = c % 2

    def out_copy():
        return copy(pc_ref.at[r], pr_ref.at[out_col], ss_o.at[0], rs_p.at[out_col], out_row, out_col)

    def share_recv(n):
        copy(pc_ref.at[0], pr_ref.at[n], ss_o.at[0], rs_p.at[n], r, c).wait_recv()

    def z_ring(step, way):
        n = 2 * ((chip + (8 - step + 1 if way == 0 else step - 1)) % 8) + core
        to = (c + (2 if way == 0 else 14)) % 16
        return copy(pr_ref.at[n], pr_ref.at[n], ss_p.at[way, step], rs_p.at[n], r, to)

    def twin_copy(k):
        n = 2 * ((chip + k) % 8) + core
        return copy(pr_ref.at[n], pr_ref.at[n], ss_t.at[k], rs_p.at[n], r, c + 1 - 2 * core)

    def stage_out():
        @pl.when(stays)
        def _():
            pr_ref[c] = pc_ref[r]

        @pl.when(jnp.logical_not(stays))
        def _():
            out_copy().start()

    def stage_share(step):
        if step == 1:
            @pl.when(jnp.logical_not(stays))
            def _():
                share_recv(c)
            twin_copy(0).start()
        else:
            share_recv(2 * ((chip + 8 - step + 1) % 8) + core)
            twin_copy(8 - step + 1).start()
            if step <= 4:
                share_recv(2 * ((chip + step - 1) % 8) + core)
                twin_copy(step - 1).start()
        if step <= 4:
            z_ring(step, 0).start()
        if step <= 3:
            z_ring(step, 1).start()

    def x_copy(m):
        rows = pl.ds((2 * m + 1 - s) * B, B)
        return copy(con_ref.at[rows], x_ref.at[m], ss_x.at[m], rs_x.at[m], (r + 4) % 8, c)

    stage_z(0)
    stage_z(1)
    stage_z(2)
    stage_y(0)
    stage_z(3)
    stage_m(1)
    stage_m(2)
    stage_m(3)
    stage_out()

    actions = {
        0: [lambda: stage_y(1)],
        1: [lambda: stage_y(2)],
        2: [lambda: stage_y(3), lambda: stage_ring(1)],
        8: [lambda: stage_share(1)],
        9: [lambda: stage_ring(2)],
        10: [lambda: stage_t(1)],
        15: [lambda: stage_share(2)],
        16: [lambda: stage_ring(3)],
        17: [lambda: stage_t(2)],
        22: [lambda: stage_share(3)],
        23: [lambda: stage_ring(4)],
        24: [lambda: stage_t(3)],
        29: [lambda: stage_share(4)],
        30: [lambda: stage_ring(5)],
        31: [lambda: x_copy(0).start(), lambda: x_copy(1).start()],
        36: [lambda: stage_share(5)],
        37: [lambda: x_copy(2).start(), lambda: x_copy(3).start()],
    }

    def block(p, carry):
        for n in range(4):
            @pl.when(p == n)
            def _():
                stage_a(n)

        def left_block(q, carry):
            def minus(j, acc):
                return acc - dot(l_ref[p, j], l_ref[q, j], 1, 1)

            acc = lax.fori_loop(0, q, minus, af[number(p, q)].reshape(B, B))
            l_ref[p, q] = dot(acc, l_ref[q, q], 1, 1)
            return carry

        lax.fori_loop(0, p, left_block, 0)

        def minus(j, acc):
            low = l_ref[p, j]
            return acc - dot(low, low, 1, 1)

        acc = lax.fori_loop(0, p, minus, af[number(p, p)].reshape(B, B))
        w_ref[...] = acc.reshape(16, 8, B)

        def tick(t):
            for n in range(4):
                if 16 * n + t in actions:
                    @pl.when(p == n)
                    def _():
                        for act in actions[16 * n + t]:
                            act()

        factor_block(w_ref, r_ref, l_ref.at[p, p], tick)
        return carry

    lax.fori_loop(0, 4, block, 0)

    for k in range(8):
        share_recv(2 * k + 1 - core)
    for p in range(4):
        for k in range(8):
            lt[p, :, k * B:(k + 1) * B] = jnp.concatenate([pr_ref[2 * n + k % 2, p, k // 2] for n in range(8)], axis=0)
        for l in range(4):
            lt[p, :, 1024 + l * B:1024 + (l + 1) * B] = pc_ref[:, p, l].reshape(B, B)
    for p in range(4):
        acc = lt[p]
        if p > 0:
            low = jnp.concatenate([l_ref[p, q] for q in range(p)], axis=1)
            acc = acc - dot(low, lt[0:p].reshape(p * B, 1536), 1, 0)
        lt[p] = dot(l_ref[p, p], acc, 1, 0)
        if p >= 2:
            for k in range(8):
                gone = jnp.logical_or(8 * k + r == pv[0], 8 * k + r == pv[1])
                kept = lt[p, :, k * B:(k + 1) * B]
                lt[p, :, k * B:(k + 1) * B] = jnp.where(gone, 0.0, kept)
        hi, lo = split(lt[p])
        rows_hi[:, p * B:(p + 1) * B] = hi[:, 0:1024].T
        rows_lo[:, p * B:(p + 1) * B] = lo[:, 0:1024].T
        cols_hi[p * B:(p + 1) * B, :] = hi[:, 1024:1536]
        cols_lo[p * B:(p + 1) * B, :] = lo[:, 1024:1536]
    lf[...] = lt[c // 4, pl.ds(pl.multiple_of((c % 4) * 32, 32), 32), 0:1024]
    lf_copy = pltpu.make_async_copy(lf, lf_any, out_sem.at[2])
    lf_copy.start()
    for m in range(4):
        x_copy(m).wait()
    row = lax.broadcasted_iota(jnp.int32, (B, B), 0)
    col = lax.broadcasted_iota(jnp.int32, (B, B), 1)
    stores = []
    for half in range(2):
        part = slice(half * 512, (half + 1) * 512)
        st[part, :] = (
            bdot(rows_hi[part, :], cols_hi[...])
            + (bdot(rows_hi[part, :], cols_lo[...]) + bdot(rows_lo[part, :], cols_hi[...]))
        )
        for m in range(4):
            k = 4 * half + m
            own = con_ref[pl.ds(pl.multiple_of((2 * m + s) * B, B), B), :]
            other = x_ref[m]
            row_gone = 8 * k + r == pv[0]
            for p in range(1, 4):
                row_gone = jnp.logical_or(row_gone, 8 * k + r == pv[p])
            own_row = cm[s, 8 * m + r] == 8 * k + r
            other_row = cm[1 - s, 8 * m + r] == 8 * k + r
            dk = jnp.where(row == col, jnp.broadcast_to(fd_ref[k:k + 1, :], (B, B)), 0.0)
            for l in range(4):
                i = l % 2
                front_col = 16 * l + c
                gone = row_gone
                for p in range(4):
                    gone = jnp.logical_or(gone, front_col == pv[p])
                own_here = jnp.logical_and(own_row, cm[s, 16 * i + c] == front_col)
                other_here = jnp.logical_and(other_row, cm[1 - s, 16 * i + c] == front_col)
                tile = jnp.where(own_here, own[:, i * B:(i + 1) * B], 0.0)
                tile = tile + jnp.where(other_here, other[:, i * B:(i + 1) * B], 0.0)
                tile = tile + jnp.where(8 * k + r == front_col, dk, 0.0)
                at = (slice(k * B, (k + 1) * B), slice(l * B, (l + 1) * B))
                st[at] = jnp.where(gone, 0.0, tile - st[at])
        store = pltpu.make_async_copy(
            st.at[pl.ds(half * 512, 512)], s_any.at[pl.ds(half * 512, 512)], out_sem.at[half]
        )
        store.start()
        stores.append(store)
    for k in range(8):
        twin_copy(k).wait_send()

    @pl.when(jnp.logical_not(stays))
    def _():
        out_copy().wait_send()
    for step in range(1, 5):
        ring(step, 0).wait_send()
        z_ring(step, 0).wait_send()
        if step <= 3:
            ring(step, 1).wait_send()
            z_ring(step, 1).wait_send()
    for p in range(4):
        for k in range(1, 8):
            rs_copy(p, k).wait_send()
    for k in range(1, 8):
        w_copy(k).wait_send()
    for k in range(1, 16):
        z_copy(k).wait_send()
    for p in range(1, 4):
        for q in range(p + 1):
            @pl.when(c != home(p, q))
            def _():
                b_copy(p, q).wait_send()

            @pl.when(c == home(p, q))
            def _():
                for k in range(1, 8):
                    y_copy(k).wait_send()
                for k in range(1, 8):
                    g_copy(p, q, k).wait_send()

            @pl.when(c % 2 == home(p, q) % 2)
            def _():
                h_copy(p, q).wait_send()
    for store in stores:
        store.wait()
    lf_copy.wait()


def factor(pv, cm, contrib, fd):
    dma = pltpu.SemaphoreType.DMA
    hbm = pl.BlockSpec(memory_space=pltpu.HBM)
    return pl.pallas_call(
        factor_kernel,
        out_shape=(
            jax.ShapeDtypeStruct((32, 1024), F32),
            jax.ShapeDtypeStruct((1024, 512), F32),
        ),
        in_specs=[hbm] * 4,
        out_specs=(hbm, hbm),
        scratch_shapes=[
            pltpu.VMEM((4, 4, B, B), F32),
            pltpu.VMEM((8, 4, 4, 16, B), F32),
            pltpu.VMEM((16, 4, 4, 16, B), F32),
            pltpu.VMEM((4, B, 256), F32),
            pltpu.VMEM((4, B, 1536), F32),
            pltpu.VMEM((1024, 512), jnp.bfloat16),
            pltpu.VMEM((1024, 512), jnp.bfloat16),
            pltpu.VMEM((512, 512), jnp.bfloat16),
            pltpu.VMEM((512, 512), jnp.bfloat16),
            pltpu.VMEM((32, 1024), F32),
            pltpu.VMEM((1024, 512), F32),
            dma((3,)),
            pltpu.SMEM((4,), jnp.int32),
            pltpu.SMEM((2, 32), jnp.int32),
            pltpu.VMEM((1024, 256), F32),
            pltpu.VMEM((8, B), F32),
            dma((4,)),
            pltpu.VMEM((8, 72, 256), F32),
            pltpu.VMEM((8, 72, 256), F32),
            pltpu.VMEM((4, 4, 16, B), F32),
            pltpu.VMEM((16, 16, B), F32),
            pltpu.VMEM((16, 16, B), F32),
            pltpu.VMEM((8, 16, B), F32),
            pltpu.VMEM((10, 8, 16, B), F32),
            pltpu.VMEM((16, 8, B), F32),
            pltpu.VMEM((16, 8, B), F32),
            dma((4, 8)), dma((4, 8)), dma((16,)), dma((16,)), dma((4, 4)), dma((16,)),
            dma((16,)), dma((4, 4)), dma((4, 4)), dma((8,)), dma((8,)), dma((8,)), dma((8,)),
            dma((2, 5)), dma((8,)), dma((1,)), dma((2, 5)), dma((16,)), dma((8,)), dma((4,)), dma((4,)),
        ],
        compiler_params=pltpu.CompilerParams(
            collective_id=0, has_side_effects=True, vmem_limit_bytes=60 << 20
        ),
        name="factor",
        cost_estimate=pl.CostEstimate(flops=200_000_000, bytes_accessed=10_000_000, transcendentals=0),
    )(pv, cm, contrib, fd)


def per_device(contrib, front_diag, child_map, pivots):
    fd = front_diag.reshape(8, B)
    lf, schur = factor(pivots, child_map, contrib, fd)
    return lf.T, schur


def solution(mesh):
    placed = (P(("front", "row"), "col"), P(("front", "row")), P("front", None), P("front"))
    return jax.shard_map(
        per_device,
        mesh=mesh,
        in_specs=placed,
        out_specs=(P(("front", "row"), "col"), P(("front", "row"), "col")),
        check_vma=False,
    )
```

```python
import jax
import jax.numpy as jnp
from jax import lax
from jax.experimental import pallas as pl
from jax.experimental.pallas import tpu as pltpu
from jax.sharding import PartitionSpec as P

F32 = jnp.float32
HIGHEST = lax.Precision.HIGHEST
MESH = pl.DeviceIdType.MESH
B = 128


def dot(a, b, ca, cb):
    return lax.dot_general(
        a, b, (((ca,), (cb,)), ((), ())), precision=HIGHEST, preferred_element_type=F32
    )


def split(x):
    high = x.astype(jnp.bfloat16)
    return high, (x - high.astype(F32)).astype(jnp.bfloat16)


def bdot(a, b):
    return lax.dot_general(a, b, (((1,), (0,)), ((), ())), preferred_element_type=F32)


def fetch(*pairs, sem):
    copies = [pltpu.make_async_copy(src, dst, sem.at[n]) for n, (src, dst) in enumerate(pairs)]
    for cp in copies:
        cp.start()
    return copies


def factor_block(w_ref, r_ref, out_ref, tick):
    row = lax.broadcasted_iota(jnp.int32, (16, 8, B), 0) * 8 + lax.broadcasted_iota(
        jnp.int32, (16, 8, B), 1
    )
    col = lax.broadcasted_iota(jnp.int32, (16, 8, B), 2)
    r_ref[...] = jnp.where(row == col, 1.0, 0.0).astype(F32)
    for t in range(16):
        tick(t)
        w = w_ref[t]
        v = r_ref[t]
        cols = [jnp.broadcast_to(w[:, 8 * t + k:8 * t + k + 1], (8, B)) for k in range(8)]
        a = [[None] * 8 for _ in range(8)]
        for k in range(8):
            for i in range(k, 8):
                a[i][k] = jnp.broadcast_to(cols[k][i:i + 1, :], (8, B))
        wr = [jnp.broadcast_to(w[i:i + 1, :], (8, B)) for i in range(8)]
        vr = [jnp.broadcast_to(v[i:i + 1, :], (8, B)) for i in range(8)]
        rs = [None] * 8
        l = [[None] * 8 for _ in range(8)]
        for k in range(8):
            rs[k] = lax.rsqrt(a[k][k])
            for i in range(k + 1, 8):
                l[i][k] = a[i][k] * rs[k]
            for j in range(k + 1, 8):
                for i in range(j, 8):
                    a[i][j] = a[i][j] - l[i][k] * l[j][k]
            wr[k] = wr[k] * rs[k]
            vr[k] = vr[k] * rs[k]
            for i in range(k + 1, 8):
                wr[i] = wr[i] - l[i][k] * wr[k]
                vr[i] = vr[i] - l[i][k] * vr[k]
        for k in range(8):
            out_ref[8 * t + k:8 * t + k + 1, :] = vr[k][0:1, :]
        if t < 15:
            for k in range(7, -1, -1):
                for i in range(k + 1, 8):
                    wr[k] = wr[k] - l[i][k] * wr[i]
                    vr[k] = vr[k] - l[i][k] * vr[i]
                wr[k] = wr[k] * rs[k]
                vr[k] = vr[k] * rs[k]
            for u in range(t + 1, 16):
                old = w_ref[u]
                new = old
                inv = r_ref[u]
                for k in range(8):
                    factor = jnp.broadcast_to(old[:, 8 * t + k:8 * t + k + 1], (8, B))
                    new = new - factor * wr[k]
                    inv = inv - factor * vr[k]
                w_ref[u] = new
                r_ref[u] = inv


def number(p, q):
    return p * (p + 1) // 2 + q


def home(p, q):
    return (number(p, q) - 1) * 2 % 16 + (number(p, q) - 1) // 8


def factor_kernel(
    pv_any, cm_any, con_any, fd_any, lf_any, s_any,
    l_ref, pc_ref, pr_ref, x_ref, lt, rows_hi, rows_lo, cols_hi, cols_lo, lf, st, out_sem, pv, cm, con_ref, fd_ref, sem, cand, rsb, acand, za, zb, ab, af, w_ref, r_ref,
    ss_a, rs_a, ss_z, rs_z, ss_b, rs_b, ss_g, rs_g, ss_h, ss_c, rs_c, ss_w, rs_w, ss_e, rs_e, ss_o, ss_p, rs_p, ss_t, ss_x, rs_x,
):
    f = lax.axis_index("front")
    r = lax.axis_index("row")
    c = lax.axis_index("col")
    s = r // 4
    d = r % 4

    def copy(src, dst, ssem, rsem, row, col):
        return pltpu.make_async_remote_copy(
            src_ref=src, dst_ref=dst, send_sem=ssem, recv_sem=rsem,
            device_id=(f, row, col), device_id_type=MESH,
        )

    fetches = fetch(
        (pv_any, pv), (cm_any, cm), (fd_any, fd_ref), (con_any, con_ref), sem=sem
    )
    barrier = pltpu.get_barrier_semaphore()
    for k in range(1, 8):
        pl.semaphore_signal(barrier, inc=1, device_id=(f, (r + k) % 8, c), device_id_type=MESH)
    for k in range(1, 16):
        pl.semaphore_signal(barrier, inc=1, device_id=(f, r, (c + k) % 16), device_id_type=MESH)
    out_row, out_col = c % 8, 2 * r + c // 8
    in_row, in_col = c // 2, r + 8 * (c % 2)
    stays = jnp.logical_and(out_row == r, out_col == c)

    @pl.when(jnp.logical_not(stays))
    def _():
        pl.semaphore_signal(barrier, inc=1, device_id=(f, out_row, out_col), device_id_type=MESH)
        pl.semaphore_signal(barrier, inc=1, device_id=(f, in_row, in_col), device_id_type=MESH)

    cand[:, 0:8, :] = jnp.zeros((8, 8, 256), F32)
    for cp in fetches:
        cp.wait()
    for p in range(4):
        b = pv[p] % 32
        mine = jnp.logical_and(cm[s, b] == pv[p], b % 4 == d)
        rows = con_ref[pl.ds((b // 4) * B, B), :]
        rows = jnp.where(mine, rows, 0.0)
        cand[:, 8 + p * 16:24 + p * 16, :] = rows.reshape(8, 16, 256)
        line = fd_ref[pl.ds(pv[p] // 8, 1), :]
        line = jnp.where(pv[p] % 8 == r, line, 0.0)
        cand[:, p:p + 1, 0:B] = jnp.broadcast_to(line[None], (8, 1, B))
    rsb[r] = cand[r]

    pl.semaphore_wait(barrier, jnp.where(stays, 22, 24))

    def span(p):
        return pl.ds(0, 24) if p == 0 else pl.ds(8 + 16 * p, 16)

    def rs_copy(p, k):
        to = (r + k) % 8
        return copy(cand.at[to, span(p)], rsb.at[r, span(p)], ss_a.at[p, k], rs_a.at[p, r], to, c)

    for p in range(4):
        for k in range(1, 8):
            rs_copy(p, k).start()

    lane = lax.broadcasted_iota(jnp.int32, (16, B), 1)
    sub = lax.broadcasted_iota(jnp.int32, (16, B), 0)
    on_diag = lane == sub + 16 * r

    def z_copy(k):
        to = (c + k) % 16
        return copy(acand.at[0, 0], za.at[c], ss_z.at[k], rs_z.at[c], r, to)

    def b_copy(p, q):
        return copy(acand.at[p, q], zb.at[c], ss_b.at[p, q], rs_b.at[c], r, home(p, q))

    def y_copy(k):
        return copy(ab.at[r], ab.at[r], ss_c.at[k], rs_c.at[r], (r + k) % 8, c)

    def g_copy(p, q, k):
        return copy(ab, af.at[number(p, q)], ss_g.at[k], rs_g.at[p, q], r, (c + 2 * k) % 16)

    def h_copy(p, q):
        block = af.at[number(p, q)]
        return copy(block, block, ss_h.at[p, q], rs_g.at[p, q], r, c + 1 - 2 * (c % 2))

    def forwards(p, q):
        return jnp.logical_and(c % 2 == home(p, q) % 2, c != home(p, q))

    def stage_t(p):
        for q in range(p + 1):
            @pl.when(forwards(p, q))
            def _():
                copy(ab, af.at[number(p, q)], ss_g.at[1], rs_g.at[p, q], r, c).wait_recv()
                h_copy(p, q).start()

    def stage_z(p):
        for k in range(1, 8):
            frm = (r + k) % 8
            copy(
                cand.at[frm, span(p)], rsb.at[frm, span(p)], ss_a.at[p, k], rs_a.at[p, frm], frm, c
            ).wait_recv()
        rows = [rsb[n, 8 + 16 * p:24 + 16 * p, :] for n in range(8)]
        sums = [
            (rows[4 * ch] + rows[4 * ch + 1]) + (rows[4 * ch + 2] + rows[4 * ch + 3])
            for ch in range(2)
        ]
        diag = jnp.sum(rsb[:, p:p + 1, 0:B], axis=0)
        dp = jnp.where(on_diag, jnp.broadcast_to(diag, (16, B)), 0.0)
        parts = []
        for l in range(4):
            i = l % 2
            total = jnp.where(16 * l + c == pv[p], dp, 0.0)
            for ch in range(2):
                here = cm[ch, 16 * i + c] == 16 * l + c
                total = total + jnp.where(here, sums[ch][:, i * B:(i + 1) * B], 0.0)
            pc_ref[r, p, l] = total
            parts.append(total)
        for q in range(p + 1):
            total = jnp.zeros((16, B), F32)
            for l in range(4):
                total = total + jnp.where(16 * l + c == pv[q], parts[l], 0.0)
            acand[p, q] = total
        if p == 0:
            za[c] = acand[0, 0]
            for k in range(1, 16):
                z_copy(k).start()
        else:
            for q in range(p + 1):
                @pl.when(c != home(p, q))
                def _():
                    b_copy(p, q).start()

                @pl.when(c == home(p, q))
                def _():
                    zb[c] = acand[p, q]

    def stage_m(p):
        for q in range(p + 1):
            @pl.when(c == home(p, q))
            def _():
                for k in range(1, 16):
                    frm = (c + k) % 16
                    copy(acand.at[p, q], zb.at[frm], ss_b.at[p, q], rs_b.at[frm], r, frm).wait_recv()
                ab[r] = jnp.sum(zb[...], axis=0)
                for k in range(1, 8):
                    y_copy(k).start()

    def wait_ab():
        for k in range(1, 8):
            frm = (r + k) % 8
            copy(ab.at[frm], ab.at[frm], ss_c.at[k], rs_c.at[frm], frm, c).wait_recv()

    def stage_y(p):
        if p == 0:
            for k in range(1, 16):
                frm = (c + k) % 16
                copy(acand.at[0, 0], za.at[frm], ss_z.at[k], rs_z.at[frm], r, frm).wait_recv()
            af[0, r] = jnp.sum(za[...], axis=0)
            for k in range(1, 8):
                w_copy(k).start()
        else:
            for q in range(p + 1):
                @pl.when(c == home(p, q))
                def _():
                    wait_ab()
                    for k in range(1, 8):
                        g_copy(p, q, k).start()
                    af[number(p, q)] = ab[...]
                    h_copy(p, q).start()

    def w_copy(k):
        return copy(af.at[0, r], af.at[0, r], ss_w.at[k], rs_w.at[r], (r + k) % 8, c)

    def stage_a(p):
        if p == 0:
            for k in range(1, 8):
                frm = (r + k) % 8
                copy(af.at[0, frm], af.at[0, frm], ss_w.at[k], rs_w.at[frm], frm, c).wait_recv()
        else:
            for q in range(p + 1):
                @pl.when(c % 2 != home(p, q) % 2)
                def _():
                    copy(ab, af.at[number(p, q)], ss_g.at[1], rs_g.at[p, q], r, c).wait_recv()

    def ring(step, way):
        origin = (r + (8 - step + 1 if way == 0 else step - 1)) % 8
        to = (r + (1 if way == 0 else 7)) % 8
        chunk = pc_ref.at[origin]
        return copy(chunk, chunk, ss_e.at[way, step], rs_e.at[origin], to, c)

    def ring_recv(origin):
        chunk = pc_ref.at[origin]
        copy(chunk, chunk, ss_e.at[0, 1], rs_e.at[origin], r, c).wait_recv()

    def stage_ring(step):
        if step > 1:
            ring_recv((r + 8 - step + 1) % 8)
            if step <= 4:
                ring_recv((r + step - 1) % 8)
        if step <= 4:
            ring(step, 0).start()
        if step <= 3:
            ring(step, 1).start()

    chip = c // 2
    core = c % 2

    def out_copy():
        return copy(pc_ref.at[r], pr_ref.at[out_col], ss_o.at[0], rs_p.at[out_col], out_row, out_col)

    def share_recv(n):
        copy(pc_ref.at[0], pr_ref.at[n], ss_o.at[0], rs_p.at[n], r, c).wait_recv()

    def z_ring(step, way):
        n = 2 * ((chip + (8 - step + 1 if way == 0 else step - 1)) % 8) + core
        to = (c + (2 if way == 0 else 14)) % 16
        return copy(pr_ref.at[n], pr_ref.at[n], ss_p.at[way, step], rs_p.at[n], r, to)

    def twin_copy(k):
        n = 2 * ((chip + k) % 8) + core
        return copy(pr_ref.at[n], pr_ref.at[n], ss_t.at[k], rs_p.at[n], r, c + 1 - 2 * core)

    def stage_out():
        @pl.when(stays)
        def _():
            pr_ref[c] = pc_ref[r]

        @pl.when(jnp.logical_not(stays))
        def _():
            out_copy().start()

    def stage_share(step):
        if step == 1:
            @pl.when(jnp.logical_not(stays))
            def _():
                share_recv(c)
            twin_copy(0).start()
        else:
            share_recv(2 * ((chip + 8 - step + 1) % 8) + core)
            twin_copy(8 - step + 1).start()
            if step <= 4:
                share_recv(2 * ((chip + step - 1) % 8) + core)
                twin_copy(step - 1).start()
        if step <= 4:
            z_ring(step, 0).start()
        if step <= 3:
            z_ring(step, 1).start()

    def x_copy(m):
        rows = pl.ds((2 * m + 1 - s) * B, B)
        return copy(con_ref.at[rows], x_ref.at[m], ss_x.at[m], rs_x.at[m], (r + 4) % 8, c)

    stage_z(0)
    stage_z(1)
    stage_z(2)
    stage_y(0)
    stage_z(3)
    stage_out()
    x_copy(0).start()
    stage_m(1)
    stage_m(2)
    stage_m(3)

    actions = {
        0: [lambda: stage_y(1)],
        1: [lambda: stage_y(2)],
        2: [lambda: stage_y(3), lambda: stage_ring(1)],
        6: [lambda: x_copy(1).start()],
        8: [lambda: stage_share(1)],
        10: [lambda: stage_t(1)],
        12: [lambda: stage_ring(2)],
        13: [lambda: x_copy(2).start()],
        17: [lambda: stage_share(2), lambda: stage_t(2)],
        21: [lambda: stage_ring(3)],
        19: [lambda: x_copy(3).start()],
        23: [lambda: stage_t(3)],
        26: [lambda: stage_share(3)],
        30: [lambda: stage_ring(4)],
        35: [lambda: stage_share(4)],
        39: [lambda: stage_ring(5)],
        43: [lambda: stage_share(5)],
    }

    def block(p, carry):
        for n in range(4):
            @pl.when(p == n)
            def _():
                stage_a(n)

        def left_block(q, carry):
            def minus(j, acc):
                return acc - dot(l_ref[p, j], l_ref[q, j], 1, 1)

            acc = lax.fori_loop(0, q, minus, af[number(p, q)].reshape(B, B))
            l_ref[p, q] = dot(acc, l_ref[q, q], 1, 1)
            return carry

        lax.fori_loop(0, p, left_block, 0)

        def minus(j, acc):
            low = l_ref[p, j]
            return acc - dot(low, low, 1, 1)

        acc = lax.fori_loop(0, p, minus, af[number(p, p)].reshape(B, B))
        w_ref[...] = acc.reshape(16, 8, B)

        def tick(t):
            for n in range(4):
                if 16 * n + t in actions:
                    @pl.when(p == n)
                    def _():
                        for act in actions[16 * n + t]:
                            act()

        factor_block(w_ref, r_ref, l_ref.at[p, p], tick)
        return carry

    lax.fori_loop(0, 4, block, 0)

    for k in range(8):
        share_recv(2 * k + 1 - core)
    for p in range(4):
        for k in range(8):
            lt[p, :, k * B:(k + 1) * B] = jnp.concatenate([pr_ref[2 * n + k % 2, p, k // 2] for n in range(8)], axis=0)
        for l in range(4):
            lt[p, :, 1024 + l * B:1024 + (l + 1) * B] = pc_ref[:, p, l].reshape(B, B)
    for p in range(4):
        acc = lt[p]
        if p > 0:
            low = jnp.concatenate([l_ref[p, q] for q in range(p)], axis=1)
            acc = acc - dot(low, lt[0:p].reshape(p * B, 1536), 1, 0)
        lt[p] = dot(l_ref[p, p], acc, 1, 0)
        if p >= 2:
            for k in range(8):
                gone = jnp.logical_or(8 * k + r == pv[0], 8 * k + r == pv[1])
                kept = lt[p, :, k * B:(k + 1) * B]
                lt[p, :, k * B:(k + 1) * B] = jnp.where(gone, 0.0, kept)
        hi, lo = split(lt[p])
        rows_hi[:, p * B:(p + 1) * B] = hi[:, 0:1024].T
        rows_lo[:, p * B:(p + 1) * B] = lo[:, 0:1024].T
        cols_hi[p * B:(p + 1) * B, :] = hi[:, 1024:1536]
        cols_lo[p * B:(p + 1) * B, :] = lo[:, 1024:1536]
    lf[...] = lt[c // 4, pl.ds(pl.multiple_of((c % 4) * 32, 32), 32), 0:1024]
    lf_copy = pltpu.make_async_copy(lf, lf_any, out_sem.at[2])
    lf_copy.start()
    for m in range(4):
        x_copy(m).wait()
    row = lax.broadcasted_iota(jnp.int32, (B, B), 0)
    col = lax.broadcasted_iota(jnp.int32, (B, B), 1)
    stores = []
    for half in range(2):
        part = slice(half * 512, (half + 1) * 512)
        st[part, :] = (
            bdot(rows_hi[part, :], cols_hi[...])
            + (bdot(rows_hi[part, :], cols_lo[...]) + bdot(rows_lo[part, :], cols_hi[...]))
        )
        for m in range(4):
            k = 4 * half + m
            own = con_ref[pl.ds(pl.multiple_of((2 * m + s) * B, B), B), :]
            other = x_ref[m]
            row_gone = 8 * k + r == pv[0]
            for p in range(1, 4):
                row_gone = jnp.logical_or(row_gone, 8 * k + r == pv[p])
            own_row = cm[s, 8 * m + r] == 8 * k + r
            other_row = cm[1 - s, 8 * m + r] == 8 * k + r
            dk = jnp.where(row == col, jnp.broadcast_to(fd_ref[k:k + 1, :], (B, B)), 0.0)
            for l in range(4):
                i = l % 2
                front_col = 16 * l + c
                gone = row_gone
                for p in range(4):
                    gone = jnp.logical_or(gone, front_col == pv[p])
                own_here = jnp.logical_and(own_row, cm[s, 16 * i + c] == front_col)
                other_here = jnp.logical_and(other_row, cm[1 - s, 16 * i + c] == front_col)
                tile = jnp.where(own_here, own[:, i * B:(i + 1) * B], 0.0)
                tile = tile + jnp.where(other_here, other[:, i * B:(i + 1) * B], 0.0)
                tile = tile + jnp.where(8 * k + r == front_col, dk, 0.0)
                at = (slice(k * B, (k + 1) * B), slice(l * B, (l + 1) * B))
                st[at] = jnp.where(gone, 0.0, tile - st[at])
        store = pltpu.make_async_copy(
            st.at[pl.ds(half * 512, 512)], s_any.at[pl.ds(half * 512, 512)], out_sem.at[half]
        )
        store.start()
        stores.append(store)
    for k in range(8):
        twin_copy(k).wait_send()

    @pl.when(jnp.logical_not(stays))
    def _():
        out_copy().wait_send()
    for step in range(1, 5):
        ring(step, 0).wait_send()
        z_ring(step, 0).wait_send()
        if step <= 3:
            ring(step, 1).wait_send()
            z_ring(step, 1).wait_send()
    for p in range(4):
        for k in range(1, 8):
            rs_copy(p, k).wait_send()
    for k in range(1, 8):
        w_copy(k).wait_send()
    for k in range(1, 16):
        z_copy(k).wait_send()
    for p in range(1, 4):
        for q in range(p + 1):
            @pl.when(c != home(p, q))
            def _():
                b_copy(p, q).wait_send()

            @pl.when(c == home(p, q))
            def _():
                for k in range(1, 8):
                    y_copy(k).wait_send()
                for k in range(1, 8):
                    g_copy(p, q, k).wait_send()

            @pl.when(c % 2 == home(p, q) % 2)
            def _():
                h_copy(p, q).wait_send()
    for store in stores:
        store.wait()
    lf_copy.wait()


def factor(pv, cm, contrib, fd):
    dma = pltpu.SemaphoreType.DMA
    hbm = pl.BlockSpec(memory_space=pltpu.HBM)
    return pl.pallas_call(
        factor_kernel,
        out_shape=(
            jax.ShapeDtypeStruct((32, 1024), F32),
            jax.ShapeDtypeStruct((1024, 512), F32),
        ),
        in_specs=[hbm] * 4,
        out_specs=(hbm, hbm),
        scratch_shapes=[
            pltpu.VMEM((4, 4, B, B), F32),
            pltpu.VMEM((8, 4, 4, 16, B), F32),
            pltpu.VMEM((16, 4, 4, 16, B), F32),
            pltpu.VMEM((4, B, 256), F32),
            pltpu.VMEM((4, B, 1536), F32),
            pltpu.VMEM((1024, 512), jnp.bfloat16),
            pltpu.VMEM((1024, 512), jnp.bfloat16),
            pltpu.VMEM((512, 512), jnp.bfloat16),
            pltpu.VMEM((512, 512), jnp.bfloat16),
            pltpu.VMEM((32, 1024), F32),
            pltpu.VMEM((1024, 512), F32),
            dma((3,)),
            pltpu.SMEM((4,), jnp.int32),
            pltpu.SMEM((2, 32), jnp.int32),
            pltpu.VMEM((1024, 256), F32),
            pltpu.VMEM((8, B), F32),
            dma((4,)),
            pltpu.VMEM((8, 72, 256), F32),
            pltpu.VMEM((8, 72, 256), F32),
            pltpu.VMEM((4, 4, 16, B), F32),
            pltpu.VMEM((16, 16, B), F32),
            pltpu.VMEM((16, 16, B), F32),
            pltpu.VMEM((8, 16, B), F32),
            pltpu.VMEM((10, 8, 16, B), F32),
            pltpu.VMEM((16, 8, B), F32),
            pltpu.VMEM((16, 8, B), F32),
            dma((4, 8)), dma((4, 8)), dma((16,)), dma((16,)), dma((4, 4)), dma((16,)),
            dma((16,)), dma((4, 4)), dma((4, 4)), dma((8,)), dma((8,)), dma((8,)), dma((8,)),
            dma((2, 5)), dma((8,)), dma((1,)), dma((2, 5)), dma((16,)), dma((8,)), dma((4,)), dma((4,)),
        ],
        compiler_params=pltpu.CompilerParams(
            collective_id=0, has_side_effects=True, vmem_limit_bytes=60 << 20
        ),
        name="factor",
        cost_estimate=pl.CostEstimate(flops=200_000_000, bytes_accessed=10_000_000, transcendentals=0),
    )(pv, cm, contrib, fd)


def per_device(contrib, front_diag, child_map, pivots):
    fd = front_diag.reshape(8, B)
    lf, schur = factor(pivots, child_map, contrib, fd)
    return lf.T, schur


def solution(mesh):
    placed = (P(("front", "row"), "col"), P(("front", "row")), P("front", None), P("front"))
    return jax.shard_map(
        per_device,
        mesh=mesh,
        in_specs=placed,
        out_specs=(P(("front", "row"), "col"), P(("front", "row"), "col")),
        check_vma=False,
    )
```

```python
import jax
import jax.numpy as jnp
from jax import lax
from jax.experimental import pallas as pl
from jax.experimental.pallas import tpu as pltpu
from jax.sharding import PartitionSpec as P

F32 = jnp.float32
HIGHEST = lax.Precision.HIGHEST
MESH = pl.DeviceIdType.MESH
B = 128


def dot(a, b, ca, cb):
    return lax.dot_general(
        a, b, (((ca,), (cb,)), ((), ())), precision=HIGHEST, preferred_element_type=F32
    )


def split(x):
    high = x.astype(jnp.bfloat16)
    return high, (x - high.astype(F32)).astype(jnp.bfloat16)


def bdot(a, b):
    return lax.dot_general(a, b, (((1,), (0,)), ((), ())), preferred_element_type=F32)


def fetch(*pairs, sem):
    copies = [pltpu.make_async_copy(src, dst, sem.at[n]) for n, (src, dst) in enumerate(pairs)]
    for cp in copies:
        cp.start()
    return copies


def factor_block(w_ref, r_ref, out_ref, tick):
    row = lax.broadcasted_iota(jnp.int32, (16, 8, B), 0) * 8 + lax.broadcasted_iota(
        jnp.int32, (16, 8, B), 1
    )
    col = lax.broadcasted_iota(jnp.int32, (16, 8, B), 2)
    r_ref[...] = jnp.where(row == col, 1.0, 0.0).astype(F32)
    for t in range(16):
        tick(t)
        w = w_ref[t]
        v = r_ref[t]
        cols = [jnp.broadcast_to(w[:, 8 * t + k:8 * t + k + 1], (8, B)) for k in range(8)]
        a = [[None] * 8 for _ in range(8)]
        for k in range(8):
            for i in range(k, 8):
                a[i][k] = jnp.broadcast_to(cols[k][i:i + 1, :], (8, B))
        wr = [jnp.broadcast_to(w[i:i + 1, :], (8, B)) for i in range(8)]
        vr = [jnp.broadcast_to(v[i:i + 1, :], (8, B)) for i in range(8)]
        rs = [None] * 8
        l = [[None] * 8 for _ in range(8)]
        for k in range(8):
            rs[k] = lax.rsqrt(a[k][k])
            for i in range(k + 1, 8):
                l[i][k] = a[i][k] * rs[k]
            for j in range(k + 1, 8):
                for i in range(j, 8):
                    a[i][j] = a[i][j] - l[i][k] * l[j][k]
            wr[k] = wr[k] * rs[k]
            vr[k] = vr[k] * rs[k]
            for i in range(k + 1, 8):
                wr[i] = wr[i] - l[i][k] * wr[k]
                vr[i] = vr[i] - l[i][k] * vr[k]
        for k in range(8):
            out_ref[8 * t + k:8 * t + k + 1, :] = vr[k][0:1, :]
        if t < 15:
            for k in range(7, -1, -1):
                for i in range(k + 1, 8):
                    wr[k] = wr[k] - l[i][k] * wr[i]
                    vr[k] = vr[k] - l[i][k] * vr[i]
                wr[k] = wr[k] * rs[k]
                vr[k] = vr[k] * rs[k]
            for u in range(t + 1, 16):
                old = w_ref[u]
                new = old
                inv = r_ref[u]
                for k in range(8):
                    factor = jnp.broadcast_to(old[:, 8 * t + k:8 * t + k + 1], (8, B))
                    new = new - factor * wr[k]
                    inv = inv - factor * vr[k]
                w_ref[u] = new
                r_ref[u] = inv


def number(p, q):
    return p * (p + 1) // 2 + q


def home(p, q):
    return (number(p, q) - 1) * 2 % 16 + (number(p, q) - 1) // 8


def factor_kernel(
    pv_any, cm_any, con_any, fd_any, lf_any, s_any,
    l_ref, pc_ref, pr_ref, x_ref, lt, rows_hi, rows_lo, cols_hi, cols_lo, lf, st, out_sem, pv, cm, con_ref, fd_ref, sem, cand, rsb, acand, za, zb, ab, af, w_ref, r_ref,
    ss_a, rs_a, ss_z, rs_z, ss_b, rs_b, ss_g, rs_g, ss_h, ss_c, rs_c, ss_w, rs_w, ss_e, rs_e, ss_o, ss_p, rs_p, ss_t, ss_x, rs_x,
):
    f = lax.axis_index("front")
    r = lax.axis_index("row")
    c = lax.axis_index("col")
    s = r // 4
    d = r % 4

    def copy(src, dst, ssem, rsem, row, col):
        return pltpu.make_async_remote_copy(
            src_ref=src, dst_ref=dst, send_sem=ssem, recv_sem=rsem,
            device_id=(f, row, col), device_id_type=MESH,
        )

    fetches = fetch(
        (pv_any, pv), (cm_any, cm), (fd_any, fd_ref), (con_any, con_ref), sem=sem
    )
    barrier = pltpu.get_barrier_semaphore()
    for k in range(1, 8):
        pl.semaphore_signal(barrier, inc=1, device_id=(f, (r + k) % 8, c), device_id_type=MESH)
    for k in range(1, 16):
        pl.semaphore_signal(barrier, inc=1, device_id=(f, r, (c + k) % 16), device_id_type=MESH)
    out_row, out_col = c % 8, 2 * r + c // 8
    in_row, in_col = c // 2, r + 8 * (c % 2)
    stays = jnp.logical_and(out_row == r, out_col == c)

    @pl.when(jnp.logical_not(stays))
    def _():
        pl.semaphore_signal(barrier, inc=1, device_id=(f, out_row, out_col), device_id_type=MESH)
        pl.semaphore_signal(barrier, inc=1, device_id=(f, in_row, in_col), device_id_type=MESH)

    cand[:, 0:8, :] = jnp.zeros((8, 8, 256), F32)
    for cp in fetches:
        cp.wait()
    for p in range(4):
        b = pv[p] % 32
        mine = jnp.logical_and(cm[s, b] == pv[p], b % 4 == d)
        rows = con_ref[pl.ds((b // 4) * B, B), :]
        rows = jnp.where(mine, rows, 0.0)
        cand[:, 8 + p * 16:24 + p * 16, :] = rows.reshape(8, 16, 256)
        line = fd_ref[pl.ds(pv[p] // 8, 1), :]
        line = jnp.where(pv[p] % 8 == r, line, 0.0)
        cand[:, p:p + 1, 0:B] = jnp.broadcast_to(line[None], (8, 1, B))
    rsb[r] = cand[r]

    pl.semaphore_wait(barrier, jnp.where(stays, 22, 24))

    def span(p):
        return pl.ds(0, 24) if p == 0 else pl.ds(8 + 16 * p, 16)

    def rs_copy(p, k):
        to = (r + k) % 8
        return copy(cand.at[to, span(p)], rsb.at[r, span(p)], ss_a.at[p, k], rs_a.at[p, r], to, c)

    for p in range(4):
        for k in range(1, 8):
            rs_copy(p, k).start()

    lane = lax.broadcasted_iota(jnp.int32, (16, B), 1)
    sub = lax.broadcasted_iota(jnp.int32, (16, B), 0)
    on_diag = lane == sub + 16 * r

    def z_copy(k):
        to = (c + k) % 16
        return copy(acand.at[0, 0], za.at[c], ss_z.at[k], rs_z.at[c], r, to)

    def b_copy(p, q):
        return copy(acand.at[p, q], zb.at[c], ss_b.at[p, q], rs_b.at[c], r, home(p, q))

    def y_copy(k):
        return copy(ab.at[r], ab.at[r], ss_c.at[k], rs_c.at[r], (r + k) % 8, c)

    def g_copy(p, q, k):
        return copy(ab, af.at[number(p, q)], ss_g.at[k], rs_g.at[p, q], r, (c + 2 * k) % 16)

    def h_copy(p, q):
        block = af.at[number(p, q)]
        return copy(block, block, ss_h.at[p, q], rs_g.at[p, q], r, c + 1 - 2 * (c % 2))

    def forwards(p, q):
        return jnp.logical_and(c % 2 == home(p, q) % 2, c != home(p, q))

    def stage_t(p):
        for q in range(p + 1):
            @pl.when(forwards(p, q))
            def _():
                copy(ab, af.at[number(p, q)], ss_g.at[1], rs_g.at[p, q], r, c).wait_recv()
                h_copy(p, q).start()

    def stage_z(p):
        for k in range(1, 8):
            frm = (r + k) % 8
            copy(
                cand.at[frm, span(p)], rsb.at[frm, span(p)], ss_a.at[p, k], rs_a.at[p, frm], frm, c
            ).wait_recv()
        rows = [rsb[n, 8 + 16 * p:24 + 16 * p, :] for n in range(8)]
        sums = [
            (rows[4 * ch] + rows[4 * ch + 1]) + (rows[4 * ch + 2] + rows[4 * ch + 3])
            for ch in range(2)
        ]
        diag = jnp.sum(rsb[:, p:p + 1, 0:B], axis=0)
        dp = jnp.where(on_diag, jnp.broadcast_to(diag, (16, B)), 0.0)
        parts = []
        for l in range(4):
            i = l % 2
            total = jnp.where(16 * l + c == pv[p], dp, 0.0)
            for ch in range(2):
                here = cm[ch, 16 * i + c] == 16 * l + c
                total = total + jnp.where(here, sums[ch][:, i * B:(i + 1) * B], 0.0)
            pc_ref[r, p, l] = total
            parts.append(total)
        for q in range(p + 1):
            total = jnp.zeros((16, B), F32)
            for l in range(4):
                total = total + jnp.where(16 * l + c == pv[q], parts[l], 0.0)
            acand[p, q] = total
        if p == 0:
            za[c] = acand[0, 0]
            for k in range(1, 16):
                z_copy(k).start()
        else:
            for q in range(p + 1):
                @pl.when(c != home(p, q))
                def _():
                    b_copy(p, q).start()

                @pl.when(c == home(p, q))
                def _():
                    zb[c] = acand[p, q]

    def stage_m(p):
        for q in range(p + 1):
            @pl.when(c == home(p, q))
            def _():
                for k in range(1, 16):
                    frm = (c + k) % 16
                    copy(acand.at[p, q], zb.at[frm], ss_b.at[p, q], rs_b.at[frm], r, frm).wait_recv()
                ab[r] = jnp.sum(zb[...], axis=0)
                for k in range(1, 8):
                    y_copy(k).start()

    def wait_ab():
        for k in range(1, 8):
            frm = (r + k) % 8
            copy(ab.at[frm], ab.at[frm], ss_c.at[k], rs_c.at[frm], frm, c).wait_recv()

    def stage_y(p):
        if p == 0:
            for k in range(1, 16):
                frm = (c + k) % 16
                copy(acand.at[0, 0], za.at[frm], ss_z.at[k], rs_z.at[frm], r, frm).wait_recv()
            af[0, r] = jnp.sum(za[...], axis=0)
            for k in range(1, 8):
                w_copy(k).start()
        else:
            for q in range(p + 1):
                @pl.when(c == home(p, q))
                def _():
                    wait_ab()
                    for k in range(1, 8):
                        g_copy(p, q, k).start()
                    af[number(p, q)] = ab[...]
                    h_copy(p, q).start()

    def w_copy(k):
        return copy(af.at[0, r], af.at[0, r], ss_w.at[k], rs_w.at[r], (r + k) % 8, c)

    def stage_a(p):
        if p == 0:
            for k in range(1, 8):
                frm = (r + k) % 8
                copy(af.at[0, frm], af.at[0, frm], ss_w.at[k], rs_w.at[frm], frm, c).wait_recv()
        else:
            for q in range(p + 1):
                @pl.when(c % 2 != home(p, q) % 2)
                def _():
                    copy(ab, af.at[number(p, q)], ss_g.at[1], rs_g.at[p, q], r, c).wait_recv()

    def ring(step, way):
        origin = (r + (8 - step + 1 if way == 0 else step - 1)) % 8
        to = (r + (1 if way == 0 else 7)) % 8
        chunk = pc_ref.at[origin]
        return copy(chunk, chunk, ss_e.at[way, step], rs_e.at[origin], to, c)

    def ring_recv(origin):
        chunk = pc_ref.at[origin]
        copy(chunk, chunk, ss_e.at[0, 1], rs_e.at[origin], r, c).wait_recv()

    def stage_ring(step):
        if step > 1:
            ring_recv((r + 8 - step + 1) % 8)
            if step <= 4:
                ring_recv((r + step - 1) % 8)
        if step <= 4:
            ring(step, 0).start()
        if step <= 3:
            ring(step, 1).start()

    chip = c // 2
    core = c % 2

    def out_copy():
        return copy(pc_ref.at[r], pr_ref.at[out_col], ss_o.at[0], rs_p.at[out_col], out_row, out_col)

    def share_recv(n):
        copy(pc_ref.at[0], pr_ref.at[n], ss_o.at[0], rs_p.at[n], r, c).wait_recv()

    def z_ring(step, way):
        n = 2 * ((chip + (8 - step + 1 if way == 0 else step - 1)) % 8) + core
        to = (c + (2 if way == 0 else 14)) % 16
        return copy(pr_ref.at[n], pr_ref.at[n], ss_p.at[way, step], rs_p.at[n], r, to)

    def twin_copy(k):
        n = 2 * ((chip + k) % 8) + core
        return copy(pr_ref.at[n], pr_ref.at[n], ss_t.at[k], rs_p.at[n], r, c + 1 - 2 * core)

    def stage_out():
        @pl.when(stays)
        def _():
            pr_ref[c] = pc_ref[r]

        @pl.when(jnp.logical_not(stays))
        def _():
            out_copy().start()

    def stage_share(step):
        if step == 1:
            @pl.when(jnp.logical_not(stays))
            def _():
                share_recv(c)
            twin_copy(0).start()
        else:
            share_recv(2 * ((chip + 8 - step + 1) % 8) + core)
            twin_copy(8 - step + 1).start()
            if step <= 4:
                share_recv(2 * ((chip + step - 1) % 8) + core)
                twin_copy(step - 1).start()
        if step <= 4:
            z_ring(step, 0).start()
        if step <= 3:
            z_ring(step, 1).start()

    def x_copy(m):
        rows = pl.ds((2 * m + 1 - s) * B, B)
        return copy(con_ref.at[rows], x_ref.at[m], ss_x.at[m], rs_x.at[m], (r + 4) % 8, c)

    stage_z(0)
    stage_z(1)
    stage_z(2)
    stage_y(0)
    stage_z(3)
    stage_m(1)
    stage_m(2)
    stage_m(3)
    stage_out()

    actions = {
        0: [lambda: stage_y(1)],
        1: [lambda: stage_y(2)],
        2: [lambda: stage_y(3), lambda: stage_ring(1)],
        6: [lambda: x_copy(0).start()],
        8: [lambda: stage_share(1)],
        10: [lambda: stage_t(1)],
        12: [lambda: stage_ring(2)],
        13: [lambda: x_copy(1).start()],
        17: [lambda: stage_share(2), lambda: stage_t(2)],
        21: [lambda: stage_ring(3)],
        22: [lambda: x_copy(2).start()],
        23: [lambda: stage_t(3)],
        26: [lambda: stage_share(3)],
        30: [lambda: stage_ring(4)],
        31: [lambda: x_copy(3).start()],
        35: [lambda: stage_share(4)],
        39: [lambda: stage_ring(5)],
        43: [lambda: stage_share(5)],
    }

    def block(p, carry):
        for n in range(4):
            @pl.when(p == n)
            def _():
                stage_a(n)

        def beside(n, count):
            return jnp.concatenate([l_ref[n, j] for j in range(count)], axis=1)

        for n in range(4):
            @pl.when(p == n)
            def _():
                for q in range(n):
                    acc = af[number(n, q)].reshape(B, B)
                    if q > 0:
                        acc = acc - dot(beside(n, q), beside(q, q), 1, 1)
                    l_ref[n, q] = dot(acc, l_ref[q, q], 1, 1)
                acc = af[number(n, n)].reshape(B, B)
                if n > 0:
                    low = beside(n, n)
                    acc = acc - dot(low, low, 1, 1)
                w_ref[...] = acc.reshape(16, 8, B)

        def tick(t):
            for n in range(4):
                if 16 * n + t in actions:
                    @pl.when(p == n)
                    def _():
                        for act in actions[16 * n + t]:
                            act()

        factor_block(w_ref, r_ref, l_ref.at[p, p], tick)
        return carry

    lax.fori_loop(0, 4, block, 0)

    for k in range(8):
        share_recv(2 * k + 1 - core)
    for p in range(4):
        for k in range(8):
            lt[p, :, k * B:(k + 1) * B] = jnp.concatenate([pr_ref[2 * n + k % 2, p, k // 2] for n in range(8)], axis=0)
        for l in range(4):
            lt[p, :, 1024 + l * B:1024 + (l + 1) * B] = pc_ref[:, p, l].reshape(B, B)
    for p in range(4):
        acc = lt[p]
        if p > 0:
            low = jnp.concatenate([l_ref[p, q] for q in range(p)], axis=1)
            acc = acc - dot(low, lt[0:p].reshape(p * B, 1536), 1, 0)
        lt[p] = dot(l_ref[p, p], acc, 1, 0)
        if p >= 2:
            for k in range(8):
                gone = jnp.logical_or(8 * k + r == pv[0], 8 * k + r == pv[1])
                kept = lt[p, :, k * B:(k + 1) * B]
                lt[p, :, k * B:(k + 1) * B] = jnp.where(gone, 0.0, kept)
        hi, lo = split(lt[p])
        rows_hi[:, p * B:(p + 1) * B] = hi[:, 0:1024].T
        rows_lo[:, p * B:(p + 1) * B] = lo[:, 0:1024].T
        cols_hi[p * B:(p + 1) * B, :] = hi[:, 1024:1536]
        cols_lo[p * B:(p + 1) * B, :] = lo[:, 1024:1536]
    lf[...] = lt[c // 4, pl.ds(pl.multiple_of((c % 4) * 32, 32), 32), 0:1024]
    lf_copy = pltpu.make_async_copy(lf, lf_any, out_sem.at[2])
    lf_copy.start()
    for m in range(4):
        x_copy(m).wait()
    row = lax.broadcasted_iota(jnp.int32, (B, B), 0)
    col = lax.broadcasted_iota(jnp.int32, (B, B), 1)
    stores = []
    for half in range(2):
        part = slice(half * 512, (half + 1) * 512)
        st[part, :] = (
            bdot(rows_hi[part, :], cols_hi[...])
            + (bdot(rows_hi[part, :], cols_lo[...]) + bdot(rows_lo[part, :], cols_hi[...]))
        )
        for m in range(4):
            k = 4 * half + m
            own = con_ref[pl.ds(pl.multiple_of((2 * m + s) * B, B), B), :]
            other = x_ref[m]
            row_gone = 8 * k + r == pv[0]
            for p in range(1, 4):
                row_gone = jnp.logical_or(row_gone, 8 * k + r == pv[p])
            own_row = cm[s, 8 * m + r] == 8 * k + r
            other_row = cm[1 - s, 8 * m + r] == 8 * k + r
            dk = jnp.where(row == col, jnp.broadcast_to(fd_ref[k:k + 1, :], (B, B)), 0.0)
            for l in range(4):
                i = l % 2
                front_col = 16 * l + c
                gone = row_gone
                for p in range(4):
                    gone = jnp.logical_or(gone, front_col == pv[p])
                own_here = jnp.logical_and(own_row, cm[s, 16 * i + c] == front_col)
                other_here = jnp.logical_and(other_row, cm[1 - s, 16 * i + c] == front_col)
                tile = jnp.where(own_here, own[:, i * B:(i + 1) * B], 0.0)
                tile = tile + jnp.where(other_here, other[:, i * B:(i + 1) * B], 0.0)
                tile = tile + jnp.where(8 * k + r == front_col, dk, 0.0)
                at = (slice(k * B, (k + 1) * B), slice(l * B, (l + 1) * B))
                st[at] = jnp.where(gone, 0.0, tile - st[at])
        store = pltpu.make_async_copy(
            st.at[pl.ds(half * 512, 512)], s_any.at[pl.ds(half * 512, 512)], out_sem.at[half]
        )
        store.start()
        stores.append(store)
    for k in range(8):
        twin_copy(k).wait_send()

    @pl.when(jnp.logical_not(stays))
    def _():
        out_copy().wait_send()
    for step in range(1, 5):
        ring(step, 0).wait_send()
        z_ring(step, 0).wait_send()
        if step <= 3:
            ring(step, 1).wait_send()
            z_ring(step, 1).wait_send()
    for p in range(4):
        for k in range(1, 8):
            rs_copy(p, k).wait_send()
    for k in range(1, 8):
        w_copy(k).wait_send()
    for k in range(1, 16):
        z_copy(k).wait_send()
    for p in range(1, 4):
        for q in range(p + 1):
            @pl.when(c != home(p, q))
            def _():
                b_copy(p, q).wait_send()

            @pl.when(c == home(p, q))
            def _():
                for k in range(1, 8):
                    y_copy(k).wait_send()
                for k in range(1, 8):
                    g_copy(p, q, k).wait_send()

            @pl.when(c % 2 == home(p, q) % 2)
            def _():
                h_copy(p, q).wait_send()
    for store in stores:
        store.wait()
    lf_copy.wait()


def factor(pv, cm, contrib, fd):
    dma = pltpu.SemaphoreType.DMA
    hbm = pl.BlockSpec(memory_space=pltpu.HBM)
    return pl.pallas_call(
        factor_kernel,
        out_shape=(
            jax.ShapeDtypeStruct((32, 1024), F32),
            jax.ShapeDtypeStruct((1024, 512), F32),
        ),
        in_specs=[hbm] * 4,
        out_specs=(hbm, hbm),
        scratch_shapes=[
            pltpu.VMEM((4, 4, B, B), F32),
            pltpu.VMEM((8, 4, 4, 16, B), F32),
            pltpu.VMEM((16, 4, 4, 16, B), F32),
            pltpu.VMEM((4, B, 256), F32),
            pltpu.VMEM((4, B, 1536), F32),
            pltpu.VMEM((1024, 512), jnp.bfloat16),
            pltpu.VMEM((1024, 512), jnp.bfloat16),
            pltpu.VMEM((512, 512), jnp.bfloat16),
            pltpu.VMEM((512, 512), jnp.bfloat16),
            pltpu.VMEM((32, 1024), F32),
            pltpu.VMEM((1024, 512), F32),
            dma((3,)),
            pltpu.SMEM((4,), jnp.int32),
            pltpu.SMEM((2, 32), jnp.int32),
            pltpu.VMEM((1024, 256), F32),
            pltpu.VMEM((8, B), F32),
            dma((4,)),
            pltpu.VMEM((8, 72, 256), F32),
            pltpu.VMEM((8, 72, 256), F32),
            pltpu.VMEM((4, 4, 16, B), F32),
            pltpu.VMEM((16, 16, B), F32),
            pltpu.VMEM((16, 16, B), F32),
            pltpu.VMEM((8, 16, B), F32),
            pltpu.VMEM((10, 8, 16, B), F32),
            pltpu.VMEM((16, 8, B), F32),
            pltpu.VMEM((16, 8, B), F32),
            dma((4, 8)), dma((4, 8)), dma((16,)), dma((16,)), dma((4, 4)), dma((16,)),
            dma((16,)), dma((4, 4)), dma((4, 4)), dma((8,)), dma((8,)), dma((8,)), dma((8,)),
            dma((2, 5)), dma((8,)), dma((1,)), dma((2, 5)), dma((16,)), dma((8,)), dma((4,)), dma((4,)),
        ],
        compiler_params=pltpu.CompilerParams(
            collective_id=0, has_side_effects=True, vmem_limit_bytes=60 << 20
        ),
        name="factor",
        cost_estimate=pl.CostEstimate(flops=200_000_000, bytes_accessed=10_000_000, transcendentals=0),
    )(pv, cm, contrib, fd)


def per_device(contrib, front_diag, child_map, pivots):
    fd = front_diag.reshape(8, B)
    lf, schur = factor(pivots, child_map, contrib, fd)
    return lf.T, schur


def solution(mesh):
    placed = (P(("front", "row"), "col"), P(("front", "row")), P("front", None), P("front"))
    return jax.shard_map(
        per_device,
        mesh=mesh,
        in_specs=placed,
        out_specs=(P(("front", "row"), "col"), P(("front", "row"), "col")),
        check_vma=False,
    )
```
